32 devices in a mesh: batch: 8 (over y, x, core), seq: 4 (over z).
Axes of the slice: x: 2, y: 2, z: 4, core: 2. Of those that a mesh axis runs over, the one named last changes fastest.
Arguments:
- tokens: bfloat16 [16, 1824, 768], P('batch', 'seq'), may hold values from -6 to 6
- cotangent: bfloat16 [16, 1824, 768], P('batch', 'seq'), may hold values from -6 to 6
- tags: int32 [16], P('batch'), may hold values from 0 to 21
- loss_weights: float32 [22], replicated, may hold values from 0.25 to 4
- w_qkv: float32 [768, 896], P('batch'), may hold values from -0.109375 to 0.109375
- m_qkv: float32 [768, 896], P('batch'), may hold values from -0.00061035156 to 0.00061035156
- v_qkv: float32 [768, 896], P('batch'), may hold values from 1.6676273e-10 to 6.670509e-10
- w_out: float32 [768, 768], P('batch'), may hold values from -1.75 to 1.75
- m_out: float32 [768, 768], P('batch'), may hold values from -0.00012207031 to 0.00012207031
- v_out: float32 [768, 768], P('batch'), may hold values from 5.8513238e-12 to 2.3405295e-11
- w_up: float32 [768, 3072], P('batch'), may hold values from -0.21650635 to 0.21650635
- m_up: float32 [768, 3072], P('batch'), may hold values from -0.00061035156 to 0.00061035156
- v_up: float32 [768, 3072], P('batch'), may hold values from 1.6676273e-10 to 6.670509e-10
- w_down: float32 [3072, 768], P('batch'), may hold values from -0.109375 to 0.109375
- m_down: float32 [3072, 768], P('batch'), may hold values from -0.00061035156 to 0.00061035156
- v_down: float32 [3072, 768], P('batch'), may hold values from 1.6676273e-10 to 6.670509e-10
- norm_params: float32 [4, 768], P(None, 'batch'), may hold values from -1 to 6, as said below
- m_norm: float32 [4, 768], P(None, 'batch'), may hold values from -0.001953125 to 0.001953125
- v_norm: float32 [4, 768], P(None, 'batch'), may hold values from 1.5008645e-09 to 6.003458e-09
Outputs:
- layer_out: bfloat16 [16, 1824, 768], P('batch', 'seq')
- input_grad: bfloat16 [16, 1824, 768], P('batch', 'seq')
- grad_norm: float32 [], replicated
- qkv_new: float32 [768, 896], P('batch')
- qkv_first: float32 [768, 896], P('batch')
- qkv_second: float32 [768, 896], P('batch')
- out_new: float32 [768, 768], P('batch')
- out_first: float32 [768, 768], P('batch')
- out_second: float32 [768, 768], P('batch')
- up_new: float32 [768, 3072], P('batch')
- up_first: float32 [768, 3072], P('batch')
- up_second: float32 [768, 3072], P('batch')
- down_new: float32 [3072, 768], P('batch')
- down_first: float32 [3072, 768], P('batch')
- down_second: float32 [3072, 768], P('batch')
- norm_new: float32 [4, 768], P(None, 'batch')
- norm_first: float32 [4, 768], P(None, 'batch')
- norm_second: float32 [4, 768], P(None, 'batch')
The draws below stay inside these ranges and needn't reach their ends.
Inputs may be any that keep to these rules, and one draw needn't show every extreme that they name: `norm_params`: rows 0 and 2 are positive gains, rows 1 and 3 biases.
All inputs are finite; a program needn't handle non-finite values.
Results may differ from the reference program's by a relative error of at most 0.0055.
The reference program's roundings to bfloat16 on the way count: a program that leaves them out, or rounds other values in their place, can miss the bound.
Values may be sent and summed in bfloat16 or wider, within the bound.
No kernel may reach another device: no remote copies, remote signals or barrier semaphores. Data moves between devices by JAX's collectives and lax.ppermute only.
A program may use at most 192 MiB of HBM per device.

```python
import math
import jax
import jax.numpy as jnp
from jax import lax

D = 768
H = 12
HD = 64
FF = 3072
ROT = 16
LEN = 1824
SEQS_DEV = 2
NSUB = 22
STEP = 10
SEQS = 16
N_BATCH = 8


def draw_norm_params(key, part):
    first, second = jax.random.split(jax.random.fold_in(key, 11), 2)
    place = jnp.arange(D).astype(jnp.float32) / D
    gain = (1.0 + 2.0 * place) * jax.random.uniform(first, (2, D), minval=0.75, maxval=1.25)
    shift = jax.random.uniform(second, (2, D), minval=-1.0, maxval=1.0)
    return jnp.stack([gain[0], shift[0], gain[1], shift[1]]).astype(jnp.float32)


def draw_w_up(key, part):
    first, second = jax.random.split(jax.random.fold_in(key, 23), 2)
    noise = jnp.clip(jax.random.normal(first, (D, FF)), -4.0, 4.0)
    common = jnp.clip(jax.random.normal(second, (1, FF)), -4.0, 4.0)
    return ((noise + 0.5 * common) * D ** (-0.5)).astype(jnp.float32)


def plant(entries, key, smallest, top_value):
    shape = entries.shape
    index_at = [jax.random.randint(jax.random.fold_in(key, axis), (), 0, shape[axis]) for axis in range(len(shape))]
    entries = entries.at[tuple(index_at)].set(smallest)
    longest = shape.index(max(shape))
    index_at[longest] = (index_at[longest] + 1) % shape[longest]
    return entries.at[tuple(index_at)].set(top_value)


def block_levels(key, dims, cuts, least, high):
    def one(axis_at, parts):
        draws = jax.random.uniform(jax.random.fold_in(jax.random.fold_in(key, 6), axis_at), (parts,), jnp.float32, least / len(cuts), high / len(cuts))
        return jnp.repeat(jnp.exp(draws), dims[axis_at] // parts).reshape((-1,) + (1,) * (len(dims) - axis_at - 1))

    loudness = one(*cuts[0])
    for cut in cuts[1:]:
        loudness = loudness * one(*cut)
    return loudness


def normal_values(key, extent, scale, reach, cuts=(), kind=jnp.bfloat16):
    values = scale * jax.random.normal(key, extent, jnp.float32)
    if cuts:
        values = values * block_levels(key, extent, cuts, -0.22, 0.18)
    return jnp.clip(values, -reach, reach).astype(kind)


def setup_inputs(seed: int = 0) -> dict:
    key_of = jax.random.split(jax.random.key(seed), 20)
    return {
        "tokens": normal_values(key_of[0], (SEQS, LEN, D), 1.0, 6.0, ((0, 8), (1, 4))),
        "cotangent": normal_values(key_of[1], (SEQS, LEN, D), 1.0, 6.0, ((0, 8), (1, 4))),
        "tags": plant(jax.random.randint(key_of[2], (SEQS,), 0, NSUB), jax.random.fold_in(key_of[2], 1), 0, NSUB - 1).astype(jnp.int32),
        "loss_weights": jnp.clip(jnp.exp(jax.random.uniform(key_of[3], (NSUB,), jnp.float32, math.log(0.25), math.log(4.0))), 0.25, 4.0),
        "w_qkv": normal_values(key_of[4], (D, D + 2 * HD), (4 * D) ** -0.5, 0.109375, ((0, 8),), jnp.float32),
        "m_qkv": normal_values(key_of[5], (D, D + 2 * HD), (0.11 * (D * (D + 2 * HD) + D * D + 2 * D * FF) ** -0.5), 0.00061035156, ((0, 8),), jnp.float32),
        "v_qkv": jnp.clip(jnp.exp(math.log(6.670509145045855e-10) - 1.3862944 * jax.random.uniform(key_of[6], (D, D + 2 * HD), jnp.float32) ** block_levels(key_of[6], (D, D + 2 * HD), ((0, 8),), -0.2, 0.2)), 1.6676272862614638e-10, 6.670509145045855e-10),
        "w_out": normal_values(key_of[7], (D, D), (D // 64) ** -0.5, 1.75, ((0, 8),), jnp.float32),
        "m_out": normal_values(key_of[8], (D, D), (0.88 * (LEN * (D * (D + 2 * HD) + D * D + 2 * D * FF)) ** -0.5), 0.00012207031, ((0, 8),), jnp.float32),
        "v_out": jnp.clip(jnp.exp(math.log(2.340529506317246e-11) - 1.3862944 * jax.random.uniform(key_of[9], (D, D), jnp.float32) ** block_levels(key_of[9], (D, D), ((0, 8),), -0.2, 0.2)), 5.851323765793115e-12, 2.340529506317246e-11),
        "w_up": draw_w_up(jax.random.fold_in(key_of[19], 71), 0),
        "m_up": normal_values(key_of[11], (D, FF), (0.11 * (D * (D + 2 * HD) + D * D + 2 * D * FF) ** -0.5), 0.00061035156, ((0, 8),), jnp.float32),
        "v_up": jnp.clip(jnp.exp(math.log(6.670509145045855e-10) - 1.3862944 * jax.random.uniform(key_of[12], (D, FF), jnp.float32) ** block_levels(key_of[12], (D, FF), ((0, 8),), -0.2, 0.2)), 1.6676272862614638e-10, 6.670509145045855e-10),
        "w_down": normal_values(key_of[13], (FF, D), FF ** -0.5, 0.109375, ((0, 8),), jnp.float32),
        "m_down": normal_values(key_of[14], (FF, D), (0.11 * (D * (D + 2 * HD) + D * D + 2 * D * FF) ** -0.5), 0.00061035156, ((0, 8),), jnp.float32),
        "v_down": jnp.clip(jnp.exp(math.log(6.670509145045855e-10) - 1.3862944 * jax.random.uniform(key_of[15], (FF, D), jnp.float32) ** block_levels(key_of[15], (FF, D), ((0, 8),), -0.2, 0.2)), 1.6676272862614638e-10, 6.670509145045855e-10),
        "norm_params": draw_norm_params(jax.random.fold_in(key_of[19], 71), 0),
        "m_norm": normal_values(key_of[17], (4, D), (0.33 * (D * (D + 2 * HD) + D * D + 2 * D * FF) ** -0.5), 0.001953125, ((1, 8),), jnp.float32),
        "v_norm": jnp.clip(jnp.exp(math.log(6.0034581750301186e-09) - 1.3862944 * jax.random.uniform(key_of[18], (4, D), jnp.float32) ** block_levels(key_of[18], (4, D), ((1, 8),), -0.2, 0.2)), 1.5008645437575296e-09, 6.0034581750301186e-09),
    }


@jax.custom_vjp
def low(v):
    return lax.optimization_barrier(v.astype(jnp.bfloat16)).astype(jnp.float32)

@jax.custom_vjp
def low_back(v):
    return v

def low_keep(v):
    return (low(v), None)

def low_pass(kept, grad):
    return (grad,)

def back_keep(v):
    return (v, None)

def back_low(kept, grad):
    return (low(grad),)
low.defvjp(low_keep, low_pass)
low_back.defvjp(back_keep, back_low)
EPS_NORM = 1e-05
BETA_ONE = 0.9
BETA_TWO = 0.999
ADAM_EPS = 1e-08
CLIP_NORM = 1.0
RATE_SMALL = 0.02
RATE_LARGE = 0.2
RATE_NORM = 1.0
DECAY = 0.1
HIGHEST = lax.Precision.HIGHEST

def layer_norm(values, gain, shift):
    mean = lax.optimization_barrier(jnp.mean(values, -1, keepdims=True))
    centered = values - mean
    scale = lax.rsqrt(lax.optimization_barrier(jnp.mean(centered * centered, -1, keepdims=True)) + EPS_NORM)
    return centered * scale * gain + shift

def rotate(values, cosine, sine):
    half = ROT // 2
    front = values[..., :ROT]
    turned = jnp.concatenate([-front[..., half:], front[..., :half]], -1)
    return jnp.concatenate([front * cosine + turned * sine, values[..., ROT:]], -1)

def angles(first, count):
    place = (first + jnp.arange(count)).astype(jnp.float32)
    inverse = 10000.0 ** (-jnp.arange(0, ROT, 2).astype(jnp.float32) / ROT)
    turn = place[:, None] * inverse[None, :]
    turn = jnp.concatenate([turn, turn], -1)
    return (jnp.cos(turn), jnp.sin(turn))

def attend(pieces):
    query, key, value = pieces
    scores = jnp.einsum('qhd,kd->hqk', query, key, precision=HIGHEST) * HD ** (-0.5)
    scores = low_back(scores)
    causal = jnp.arange(LEN)[:, None] >= jnp.arange(LEN)[None, :]
    scores = jnp.where(causal[None], scores, -1e+30)
    weights = low(jax.nn.softmax(scores, -1))
    return jnp.einsum('hqk,kd->qhd', weights, value, precision=HIGHEST)

def layer(tokens, masters, cosine, sine):
    w_qkv, w_out, w_up, w_down, params = [low(w) for w in masters]
    count = tokens.shape[0]
    first = low(layer_norm(tokens, params[0], params[1]))
    mixed = low_back(jnp.dot(first, w_qkv, precision=HIGHEST))
    query = mixed[..., :D].reshape(count, LEN, H, HD)
    key = mixed[..., D:D + HD]
    value = mixed[..., D + HD:]
    query = low_back(low(rotate(query, cosine[:, None, :], sine[:, None, :])))
    key = low_back(low(rotate(key, cosine, sine)))
    value = low_back(low(value))
    heads = lax.map(jax.checkpoint(attend), (query, key, value))
    heads = low_back(low(heads.reshape(count, LEN, D)))
    attention = low_back(jnp.dot(heads, w_out, precision=HIGHEST))
    second = low(layer_norm(tokens, params[2], params[3]))
    up_pre = low_back(jnp.dot(second, w_up, precision=HIGHEST))
    active = low(jax.nn.gelu(up_pre, approximate=False))
    feed = low_back(jnp.dot(active, w_down, precision=HIGHEST))
    return tokens + attention + feed

def adam_update(weight, first, second, grad, rate, decay):
    first_new = BETA_ONE * first + (1.0 - BETA_ONE) * grad
    second_new = BETA_TWO * second + (1.0 - BETA_TWO) * grad * grad
    step_one = first_new / (1.0 - BETA_ONE ** STEP)
    step_two = second_new / (1.0 - BETA_TWO ** STEP)
    weight_new = weight - rate * (step_one / (jnp.sqrt(step_two) + ADAM_EPS) + decay * weight)
    return (weight_new, first_new, second_new)

def reference(tokens, cotangent, tags, loss_weights, w_qkv, m_qkv, v_qkv, w_out, m_out, v_out, w_up, m_up, v_up, w_down, m_down, v_down, norm_params, m_norm, v_norm):
    masters = (w_qkv, w_out, w_up, w_down, norm_params)
    cosine, sine = angles(0, LEN)
    row_weight = loss_weights[tags]
    groups = tokens.astype(jnp.float32).reshape(N_BATCH, SEQS_DEV, LEN, D)
    backs = (cotangent.astype(jnp.float32) * row_weight[:, None, None]).reshape(N_BATCH, SEQS_DEV, LEN, D)

    def group_step(total, pieces):
        part_tokens, part_back = pieces
        output, pull = jax.vjp(lambda t, w: layer(t, w, cosine, sine), part_tokens, masters)
        grad_tokens, grad_weights = pull(part_back)
        total = jax.tree.map(jnp.add, total, grad_weights)
        return (total, (output.astype(jnp.bfloat16), grad_tokens.astype(jnp.bfloat16)))
    zeros = jax.tree.map(jnp.zeros_like, masters)
    grads, (outputs, grad_in) = lax.scan(group_step, zeros, (groups, backs))
    squares = jnp.float32(0.0)
    for grad in grads:
        squares = squares + jnp.sum(grad * grad)
    grad_norm = jnp.sqrt(squares)
    factor = CLIP_NORM / jnp.maximum(grad_norm, CLIP_NORM)
    firsts = (m_qkv, m_out, m_up, m_down, m_norm)
    seconds = (v_qkv, v_out, v_up, v_down, v_norm)
    rates = (RATE_SMALL, RATE_LARGE, RATE_SMALL, RATE_SMALL, RATE_NORM)
    decays = (DECAY, DECAY, DECAY, DECAY, 0.0)
    results = []
    for index in range(5):
        results.extend(adam_update(masters[index], firsts[index], seconds[index], grads[index] * factor, rates[index], decays[index]))
    layer_out = outputs.reshape(SEQS, LEN, D)
    input_grad = grad_in.reshape(SEQS, LEN, D)
    return (layer_out, input_grad, grad_norm, results[0], results[1], results[2], results[3], results[4], results[5], results[6], results[7], results[8], results[9], results[10], results[11], results[12], results[13], results[14])
```

```python
import functools

import jax
import jax.numpy as jnp
from jax import lax
from jax.experimental import pallas as pl
from jax.experimental.pallas import tpu as pltpu
from jax.sharding import PartitionSpec as P

D = 768
H = 12
HD = 64
ROT = 16
STEP = 10


EPS_NORM = 1e-05
BETA_ONE = 0.9
BETA_TWO = 0.999
ADAM_EPS = 1e-08
CLIP_NORM = 1.0
RATE_SMALL = 0.02
RATE_LARGE = 0.2
RATE_NORM = 1.0
DECAY = 0.1
ROWS_FIRST = (((0,), (0,)), ((), ()))
COLS_LAST = (((1,), (1,)), ((), ()))


def layer_norm_parts(values, gain, shift):
    mean = jnp.mean(values, -1, keepdims=True)
    centered = values - mean
    scale = lax.rsqrt(jnp.mean(centered * centered, -1, keepdims=True) + EPS_NORM)
    normed = centered * scale
    return (normed, scale, normed * gain + shift)


def norm_back(grad_out, normed, scale, gain):
    grad_normed = grad_out * gain
    inner = jnp.mean(grad_normed, -1, keepdims=True)
    along = jnp.mean(grad_normed * normed, -1, keepdims=True)
    return scale * (grad_normed - inner - normed * along)


def rotate(values, cosine, sine):
    half = ROT // 2
    front = values[..., :ROT]
    turned = jnp.concatenate([-front[..., half:], front[..., :half]], -1)
    return jnp.concatenate([front * cosine + turned * sine, values[..., ROT:]], -1)


def angles(first, count):
    place = (first + jnp.arange(count)).astype(jnp.float32)
    inverse = 10000.0 ** (-jnp.arange(0, ROT, 2).astype(jnp.float32) / ROT)
    turn = place[:, None] * inverse[None, :]
    turn = jnp.concatenate([turn, turn], -1)
    return (jnp.cos(turn), jnp.sin(turn))


def adam_update(weight, first, second, grad, rate, decay):
    first_new = BETA_ONE * first + (1.0 - BETA_ONE) * grad
    second_new = BETA_TWO * second + (1.0 - BETA_TWO) * grad * grad
    step_one = first_new / (1.0 - BETA_ONE**STEP)
    step_two = second_new / (1.0 - BETA_TWO**STEP)
    weight_new = weight - rate * (step_one / (jnp.sqrt(step_two) + ADAM_EPS) + decay * weight)
    return (weight_new, first_new, second_new)


BF = jnp.bfloat16
F32 = jnp.float32
ROWS = 128
KEYS = 256


def attention_body(
    place,
    q_ref,
    do_ref,
    kv_ref,
    o_ref,
    dq_ref,
    dkv_ref,
    k_rows,
    v_rows,
    k_cols,
    v_cols,
    scores,
    out_acc,
    dq_acc,
    dkv_acc,
    *,
    local,
):
    step = pl.program_id(1)
    chunks = scores.shape[0]
    wide = H * ROWS

    @pl.when(step == 0)
    def _():
        def prepare(j, carry):
            rows = pl.ds(pl.multiple_of(j * KEYS, KEYS), KEYS)
            pair = kv_ref[0, rows, :]
            k_rows[rows, :] = pair[:, :HD]
            v_rows[rows, :] = pair[:, HD:]
            turned = pair.T
            k_cols[j] = turned[:HD]
            v_cols[j] = turned[HD:]
            dkv_acc[rows, :] = jnp.zeros((KEYS, 2 * HD), F32)
            return carry

        lax.fori_loop(0, chunks, prepare, 0)

    start = place[0] * local + step * ROWS
    last = jnp.minimum(start + ROWS - 1, (place[0] + 1) * local - 1)
    open_chunks = (start + 1) // KEYS
    all_chunks = last // KEYS + 1

    def heads_in_columns(x):
        turned = [x[:, 2 * HD * p : 2 * HD * (p + 1)].T for p in range(H // 2)]
        return jnp.concatenate([t[a : a + HD] for t in turned for a in (0, HD)], 1)

    def heads_in_rows(x):
        return jnp.concatenate([x[:, HD * h : HD * (h + 1)] for h in range(H)], 0)

    def heads_side_by_side(t):
        return jnp.concatenate(
            [
                jnp.concatenate(
                    [
                        t[:, 2 * p * ROWS : (2 * p + 1) * ROWS],
                        t[:, (2 * p + 1) * ROWS : (2 * p + 2) * ROWS],
                    ],
                    0,
                ).T
                for p in range(H // 2)
            ],
            1,
        )

    q = q_ref[0]
    do = do_ref[0]
    q_cols = heads_in_columns(q)
    do_cols = heads_in_columns(do)
    blank = jnp.zeros((wide, HD), BF)
    q_side = jnp.concatenate([heads_in_rows(q), blank], 1)
    do_side = jnp.concatenate([blank, heads_in_rows(do)], 1)
    out_acc[...] = jnp.zeros_like(out_acc)
    dq_acc[...] = jnp.zeros_like(dq_acc)
    lane = lax.broadcasted_iota(jnp.int32, (1, wide), 1)
    query_at = start + (lane & (ROWS - 1))

    def score_pass(masked):
        def one(j, top):
            rows = pl.ds(pl.multiple_of(j * KEYS, KEYS), KEYS)
            raw = jnp.dot(k_rows[rows, :], q_cols, preferred_element_type=F32)
            if masked:
                key_at = j * KEYS + lax.broadcasted_iota(jnp.int32, (KEYS, wide), 0)
                raw = jnp.where(key_at <= query_at, raw, -1e30)
            scores[j] = raw
            return jnp.maximum(top, jnp.max(raw.reshape(KEYS // 8, 8, wide), 0))

        return one

    top = jnp.full((8, wide), -1e30, F32)
    top = lax.fori_loop(0, open_chunks, score_pass(False), top)
    top = lax.fori_loop(open_chunks, all_chunks, score_pass(True), top)
    top = jnp.max(top, 0, keepdims=True)

    def value_pass(j, total):
        expo = jnp.exp(scores[j] - top)
        scores[j] = expo
        out_acc[...] += jnp.dot(v_cols[j], expo.astype(BF), preferred_element_type=F32)
        return total + jnp.sum(expo.reshape(KEYS // 8, 8, wide), 0)

    total = lax.fori_loop(0, all_chunks, value_pass, jnp.zeros((8, wide), F32))
    share = 1.0 / jnp.sum(total, 0, keepdims=True)
    out = out_acc[...] * share
    inner = jnp.sum(out * do_cols.astype(F32), 0, keepdims=True)

    def back_pass(j, carry):
        rows = pl.ds(pl.multiple_of(j * KEYS, KEYS), KEYS)
        grad_probs = jnp.dot(v_rows[rows, :], do_cols, preferred_element_type=F32)
        probs = scores[j] * share
        grad_scores = (probs * (grad_probs - inner)).astype(BF)
        dkv_acc[rows, :] += jnp.dot(
            grad_scores, q_side, preferred_element_type=F32
        ) + jnp.dot(probs.astype(BF), do_side, preferred_element_type=F32)
        dq_acc[...] += jnp.dot(k_cols[j], grad_scores, preferred_element_type=F32)
        return carry

    lax.fori_loop(0, all_chunks, back_pass, 0)
    o_ref[0] = heads_side_by_side(out).astype(BF)
    dq_ref[0] = (heads_side_by_side(dq_acc[...]) * HD ** (-0.5)).astype(BF)

    @pl.when(step == pl.num_programs(1) - 1)
    def _():
        dkv_ref[0] = dkv_acc[...].astype(BF)


def attention(place, q, do, kv, local):
    batch, rows, _ = q.shape
    keys = kv.shape[1]
    chunks = keys // KEYS
    wide = H * ROWS
    by_row = pl.BlockSpec((1, ROWS, D), lambda b, i, p: (b, i, 0))
    by_seq = pl.BlockSpec((1, keys, 2 * HD), lambda b, i, p: (b, 0, 0))
    return pl.pallas_call(
        functools.partial(attention_body, local=local),
        grid_spec=pltpu.PrefetchScalarGridSpec(
            num_scalar_prefetch=1,
            grid=(batch, rows // ROWS),
            in_specs=[by_row, by_row, by_seq],
            out_specs=[by_row, by_row, by_seq],
            scratch_shapes=[
                pltpu.VMEM((keys, HD), BF),
                pltpu.VMEM((keys, HD), BF),
                pltpu.VMEM((chunks, HD, KEYS), BF),
                pltpu.VMEM((chunks, HD, KEYS), BF),
                pltpu.VMEM((chunks, KEYS, wide), F32),
                pltpu.VMEM((HD, wide), F32),
                pltpu.VMEM((HD, wide), F32),
                pltpu.VMEM((keys, 2 * HD), F32),
            ],
        ),
        out_shape=[
            jax.ShapeDtypeStruct(q.shape, BF),
            jax.ShapeDtypeStruct(q.shape, BF),
            jax.ShapeDtypeStruct(kv.shape, BF),
        ],
        compiler_params=pltpu.CompilerParams(
            dimension_semantics=("arbitrary", "arbitrary"), vmem_limit_bytes=48 << 20
        ),
    )(place, q, do, kv)


def shift(x, by, count):
    return lax.ppermute(x, "seq", [(s, s + by) for s in range(count) if 0 <= s + by < count])


def shards(
    tokens,
    cotangent,
    tags,
    loss_weights,
    w_qkv,
    m_qkv,
    v_qkv,
    w_out,
    m_out,
    v_out,
    w_up,
    m_up,
    v_up,
    w_down,
    m_down,
    v_down,
    norm_params,
    m_norm,
    v_norm,
):
    seq_count = lax.axis_size("seq")
    seq_at = lax.axis_index("seq")
    seq_rows, local_len, width = tokens.shape
    count = seq_rows * local_len
    part = w_qkv.shape[0]

    small = jnp.concatenate(
        [w_qkv[:, D:], norm_params.T, jnp.zeros((part, 2 * HD - 4), F32)], 1
    ).astype(BF)
    small = lax.all_gather(small, "batch", axis=0, tiled=True)
    middle = jnp.concatenate([w_qkv[:, :D], w_out], 1).astype(BF)
    middle = lax.all_gather(middle, "batch", axis=0, tiled=True)
    full_up = lax.all_gather(w_up.astype(BF), "batch", axis=0, tiled=True)
    full_down = lax.all_gather(w_down.astype(BF), "batch", axis=0, tiled=True)
    full_kv = small[:, : 2 * HD]
    gains = small[:, 2 * HD : 2 * HD + 4].T.astype(F32)
    full_q = middle[:, :D]
    full_out = middle[:, D:]

    flat = tokens.astype(F32).reshape(count, width)
    normed_one, scale_one, first = layer_norm_parts(flat, gains[0], gains[1])
    first_low = first.astype(BF)
    _, _, second = layer_norm_parts(flat, gains[2], gains[3])
    second_low = second.astype(BF)

    cosine, sine = angles(seq_at * local_len, local_len)
    cos_tok = jnp.tile(cosine, (seq_rows, 1))
    sin_tok = jnp.tile(sine, (seq_rows, 1))

    mixed_kv = jnp.dot(first_low, full_kv, preferred_element_type=F32)
    key_rot = rotate(mixed_kv[:, :HD], cos_tok, sin_tok)
    pair = jnp.concatenate([key_rot, mixed_kv[:, HD:]], -1).astype(BF)
    pair = pair.reshape(seq_rows, local_len, 2 * HD)
    arrived = [pair] + [shift(pair, by, seq_count) for by in range(1, seq_count)]
    pairs = []
    for owner in range(seq_count):
        piece = jnp.zeros_like(pair)
        for by in range(seq_count):
            piece = jnp.where(seq_at - by == owner, arrived[by], piece)
        pairs.append(piece)
    keys = -(-seq_count * local_len // KEYS) * KEYS
    pairs.append(jnp.zeros((seq_rows, keys - seq_count * local_len, 2 * HD), BF))
    pairs = jnp.concatenate(pairs, 1)

    mixed_q = jnp.dot(first_low, full_q, preferred_element_type=F32)
    query = rotate(mixed_q.reshape(count, H, HD), cos_tok[:, None, :], sin_tok[:, None, :])
    query = query.reshape(seq_rows, local_len, D).astype(BF) * BF(HD ** (-0.5))
    subsets = jnp.arange(loss_weights.shape[0])
    row_weight = jnp.sum(
        jnp.where(tags[:, None] == subsets[None, :], loss_weights[None, :], 0.0), -1
    )
    grad_y = (cotangent.astype(F32) * row_weight[:, None, None]).reshape(count, D)
    grad_low = grad_y.astype(BF)
    grad_heads = (
        lax.dot_general(grad_low, full_out, COLS_LAST, preferred_element_type=F32)
        .astype(BF)
        .reshape(seq_rows, local_len, D)
    )
    rows = -(-local_len // ROWS) * ROWS
    pad = ((0, 0), (0, rows - local_len), (0, 0))
    heads, grad_query, grad_pairs = attention(
        jnp.reshape(seq_at, (1,)).astype(jnp.int32),
        jnp.pad(query, pad),
        jnp.pad(grad_heads, pad),
        pairs,
        local_len,
    )
    heads = heads[:, :local_len].reshape(count, D)
    grad_query = grad_query[:, :local_len].reshape(count, D)

    def piece_for(by):
        at = jnp.maximum(seq_at - by, 0) * local_len
        return lax.dynamic_slice_in_dim(grad_pairs, at, local_len, 1)

    grad_pair = piece_for(0).astype(F32)
    for by in range(1, seq_count):
        grad_pair = grad_pair + shift(piece_for(by), -by, seq_count).astype(F32)
    grad_pair = grad_pair.astype(BF).astype(F32).reshape(count, 2 * HD)

    up_pre = jnp.dot(second_low, full_up, preferred_element_type=F32)
    active, gelu_back = jax.vjp(lambda values: jax.nn.gelu(values, approximate=False), up_pre)
    active_low = active.astype(BF)
    attention_out = jnp.dot(heads, full_out, preferred_element_type=F32)
    feed = jnp.dot(active_low, full_down, preferred_element_type=F32)
    layer_out = (flat + attention_out + feed).astype(BF).reshape(seq_rows, local_len, D)
    grad_down = lax.dot_general(active_low, grad_low, ROWS_FIRST, preferred_element_type=F32)
    grad_active = lax.dot_general(grad_low, full_down, COLS_LAST, preferred_element_type=F32)
    grad_up_pre = gelu_back(grad_active)[0].astype(BF)
    grad_up = lax.dot_general(second_low, grad_up_pre, ROWS_FIRST, preferred_element_type=F32)
    grad_second = lax.dot_general(grad_up_pre, full_up, COLS_LAST, preferred_element_type=F32)

    grad_out_w = lax.dot_general(heads, grad_low, ROWS_FIRST, preferred_element_type=F32)
    grad_query = rotate(
        grad_query.astype(F32).reshape(count, H, HD),
        cos_tok[:, None, :],
        -sin_tok[:, None, :],
    )
    grad_key = rotate(grad_pair[:, :HD], cos_tok, -sin_tok)
    grad_mixed = jnp.concatenate(
        [grad_query.reshape(count, D), grad_key, grad_pair[:, HD:]], -1
    ).astype(BF)
    full_qkv = jnp.concatenate([full_q, full_kv], 1)
    grad_qkv = lax.dot_general(first_low, grad_mixed, ROWS_FIRST, preferred_element_type=F32)
    grad_first = lax.dot_general(grad_mixed, full_qkv, COLS_LAST, preferred_element_type=F32)
    normed_two, scale_two, _ = layer_norm_parts(flat, gains[2], gains[3])
    grad_input = (
        grad_y
        + norm_back(grad_first, normed_one, scale_one, gains[0])
        + norm_back(grad_second, normed_two, scale_two, gains[2])
    )
    input_grad = grad_input.astype(BF).reshape(seq_rows, local_len, D)
    grad_norm_params = jnp.stack(
        [
            jnp.sum(grad_first * normed_one, 0),
            jnp.sum(grad_first, 0),
            jnp.sum(grad_second * normed_two, 0),
            jnp.sum(grad_second, 0),
        ]
    )

    tail = jnp.concatenate(
        [grad_qkv, grad_out_w, grad_norm_params.T, jnp.zeros((D, 2 * HD - 4), F32)], 1
    )
    sums = [
        lax.psum_scatter(g, "batch", scatter_dimension=0, tiled=True)
        for g in (grad_down.astype(BF), grad_up.astype(BF), tail)
    ]
    sum_down, sum_up, tail = [lax.psum(g, "seq").astype(F32) for g in sums]
    qkv_width = w_qkv.shape[1]
    summed = (
        tail[:, :qkv_width],
        tail[:, qkv_width : qkv_width + D],
        sum_up,
        sum_down,
        tail[:, qkv_width + D : qkv_width + D + 4].T,
    )
    local_squares = jnp.float32(0.0)
    for grad in summed:
        local_squares = local_squares + jnp.sum(grad * grad)
    total_squares = lax.psum(local_squares, "batch")
    grad_norm = jnp.sqrt(total_squares)
    factor = CLIP_NORM / jnp.maximum(grad_norm, CLIP_NORM)
    masters = (w_qkv, w_out, w_up, w_down, norm_params)
    firsts = (m_qkv, m_out, m_up, m_down, m_norm)
    seconds = (v_qkv, v_out, v_up, v_down, v_norm)
    rates = (RATE_SMALL, RATE_LARGE, RATE_SMALL, RATE_SMALL, RATE_NORM)
    decays = (DECAY, DECAY, DECAY, DECAY, 0.0)
    results = []
    for index in range(5):
        results.extend(
            adam_update(
                masters[index],
                firsts[index],
                seconds[index],
                summed[index] * factor,
                rates[index],
                decays[index],
            )
        )
    return (layer_out, input_grad, grad_norm, *results)


def solution(mesh):
    in_specs = (
        P("batch", "seq", None),
        P("batch", "seq", None),
        P("batch"),
        P(),
        P("batch", None),
        P("batch", None),
        P("batch", None),
        P("batch", None),
        P("batch", None),
        P("batch", None),
        P("batch", None),
        P("batch", None),
        P("batch", None),
        P("batch", None),
        P("batch", None),
        P("batch", None),
        P(None, "batch"),
        P(None, "batch"),
        P(None, "batch"),
    )
    out_specs = (
        P("batch", "seq", None),
        P("batch", "seq", None),
        P(),
        P("batch", None),
        P("batch", None),
        P("batch", None),
        P("batch", None),
        P("batch", None),
        P("batch", None),
        P("batch", None),
        P("batch", None),
        P("batch", None),
        P("batch", None),
        P("batch", None),
        P("batch", None),
        P(None, "batch"),
        P(None, "batch"),
        P(None, "batch"),
    )
    return jax.shard_map(shards, mesh=mesh, in_specs=in_specs, out_specs=out_specs, check_vma=False)
```

```python
import functools
import math

import jax
import jax.numpy as jnp
from jax import lax
from jax.experimental import pallas as pl
from jax.experimental.pallas import tpu as pltpu
from jax.sharding import PartitionSpec as P

D = 768
H = 12
HD = 64
ROT = 16
STEP = 10


EPS_NORM = 1e-05
BETA_ONE = 0.9
BETA_TWO = 0.999
ADAM_EPS = 1e-08
CLIP_NORM = 1.0
RATE_SMALL = 0.02
RATE_LARGE = 0.2
RATE_NORM = 1.0
DECAY = 0.1
ROWS_FIRST = (((0,), (0,)), ((), ()))
COLS_LAST = (((1,), (1,)), ((), ()))


def angles(first, count):
    place = (first + jnp.arange(count)).astype(jnp.float32)
    inverse = 10000.0 ** (-jnp.arange(0, ROT, 2).astype(jnp.float32) / ROT)
    turn = place[:, None] * inverse[None, :]
    turn = jnp.concatenate([turn, turn], -1)
    return (jnp.cos(turn), jnp.sin(turn))


def adam_update(weight, first, second, grad, rate, decay):
    first_new = BETA_ONE * first + (1.0 - BETA_ONE) * grad
    second_new = BETA_TWO * second + (1.0 - BETA_TWO) * grad * grad
    step_one = first_new / (1.0 - BETA_ONE**STEP)
    step_two = second_new / (1.0 - BETA_TWO**STEP)
    weight_new = weight - rate * (step_one / (jnp.sqrt(step_two) + ADAM_EPS) + decay * weight)
    return (weight_new, first_new, second_new)


BF = jnp.bfloat16
F32 = jnp.float32
ROWS = 128
KEYS = 384
VMEM_BYTES = 60 << 20


def attention_body(
    place,
    q_ref,
    do_ref,
    *refs,
    local,
    devices,
):
    kv_refs, refs = refs[:devices], refs[-10 - devices :]
    o_ref, dq_ref, dkv_refs = refs[0], refs[1], refs[2 : 2 + devices]
    k_rows, v_rows, k_cols, v_cols, scores, out_acc, dq_acc, dkv_acc = refs[-8:]
    step = pl.program_id(0)
    chunks = scores.shape[0]
    wide = H * ROWS

    @pl.when(step == 0)
    def _():
        dkv_acc[...] = jnp.zeros_like(dkv_acc)
        for by, kv_ref in enumerate(kv_refs):

            @pl.when(place[0] >= by)
            def _(by=by, kv_ref=kv_ref):
                rows = pl.ds(pl.multiple_of((place[0] - by) * local, 8), local)
                dkv_acc[rows, :] = kv_ref[...].astype(F32)

        def prepare(j, carry):
            rows = pl.ds(pl.multiple_of(j * KEYS, KEYS), KEYS)
            pair = dkv_acc[rows, :].astype(BF)
            k_rows[rows, :] = pair[:, :HD]
            v_rows[rows, :] = pair[:, HD:]
            turned = pair.T
            k_cols[j] = turned[:HD]
            v_cols[j] = turned[HD:]
            dkv_acc[rows, :] = jnp.zeros((KEYS, 2 * HD), F32)
            return carry

        lax.fori_loop(0, chunks, prepare, 0)

    start = place[0] * local + step * ROWS
    last = jnp.minimum(start + ROWS - 1, (place[0] + 1) * local - 1)
    open_chunks = (start + 1) // KEYS
    all_chunks = last // KEYS + 1

    def heads_in_columns(x):
        turned = [x[:, 2 * HD * p : 2 * HD * (p + 1)].T for p in range(H // 2)]
        return jnp.concatenate([t[a : a + HD] for t in turned for a in (0, HD)], 1)

    def heads_in_rows(x):
        return jnp.concatenate([x[:, HD * h : HD * (h + 1)] for h in range(H)], 0)

    def heads_side_by_side(t):
        return jnp.concatenate(
            [
                jnp.concatenate(
                    [
                        t[:, 2 * p * ROWS : (2 * p + 1) * ROWS],
                        t[:, (2 * p + 1) * ROWS : (2 * p + 2) * ROWS],
                    ],
                    0,
                ).T
                for p in range(H // 2)
            ],
            1,
        )

    real = lax.broadcasted_iota(jnp.int32, (ROWS, D), 0) < local - step * ROWS
    q = jnp.where(real, q_ref[0], 0.0).astype(BF)
    do = jnp.where(real, do_ref[0], 0.0).astype(BF)
    q_cols = heads_in_columns(q)
    do_cols = heads_in_columns(do)
    blank = jnp.zeros((wide, HD), BF)
    q_side = jnp.concatenate([heads_in_rows(q), blank], 1)
    do_side = jnp.concatenate([blank, heads_in_rows(do)], 1)
    out_acc[...] = jnp.zeros_like(out_acc)
    dq_acc[...] = jnp.zeros_like(dq_acc)
    lane = lax.broadcasted_iota(jnp.int32, (1, wide), 1)
    query_at = start + (lane & (ROWS - 1))

    open_pairs, all_pairs, odd = open_chunks // 2, all_chunks // 2, all_chunks % 2

    def key_rows(j, count):
        return pl.ds(pl.multiple_of(j * KEYS, KEYS), count * KEYS)

    def columns(ref, j, count):
        return jnp.concatenate([ref[j + c] for c in range(count)], 1)

    def score_step(j, top, count, masked):
        raw = jnp.dot(k_rows[key_rows(j, count), :], q_cols, preferred_element_type=F32)
        if masked:
            key_at = j * KEYS + lax.broadcasted_iota(jnp.int32, (count * KEYS, wide), 0)
            raw = jnp.where(key_at <= query_at, raw, -1e30)
        scores[pl.ds(j, count)] = raw.reshape(count, KEYS, wide)
        return jnp.maximum(top, jnp.max(raw.reshape(count * KEYS // 8, 8, wide), 0))

    def value_step(j, total, count):
        expo = jnp.exp(scores[pl.ds(j, count)].reshape(count * KEYS, wide) - top)
        scores[pl.ds(j, count)] = expo.reshape(count, KEYS, wide)
        out_acc[...] += jnp.dot(
            columns(v_cols, j, count), expo.astype(BF), preferred_element_type=F32
        )
        return total + jnp.sum(expo.reshape(count * KEYS // 8, 8, wide), 0)

    def back_step(j, count):
        rows = key_rows(j, count)
        grad_probs = jnp.dot(v_rows[rows, :], do_cols, preferred_element_type=F32)
        probs = scores[pl.ds(j, count)].reshape(count * KEYS, wide) * share
        grad_scores = (probs * (grad_probs - inner)).astype(BF)
        dkv_acc[rows, :] += jnp.dot(
            grad_scores, q_side, preferred_element_type=F32
        ) + jnp.dot(probs.astype(BF), do_side, preferred_element_type=F32)
        dq_acc[...] += jnp.dot(
            columns(k_cols, j, count), grad_scores, preferred_element_type=F32
        )

    top = jnp.full((8, wide), -1e30, F32)
    top = lax.fori_loop(0, open_pairs, lambda p, t: score_step(2 * p, t, 2, False), top)
    top = lax.fori_loop(open_pairs, all_pairs, lambda p, t: score_step(2 * p, t, 2, True), top)
    top = lax.fori_loop(0, odd, lambda p, t: score_step(2 * all_pairs, t, 1, True), top)
    top = jnp.max(top, 0, keepdims=True)

    total = jnp.zeros((8, wide), F32)
    total = lax.fori_loop(0, all_pairs, lambda p, t: value_step(2 * p, t, 2), total)
    total = lax.fori_loop(0, odd, lambda p, t: value_step(2 * all_pairs, t, 1), total)
    share = 1.0 / jnp.sum(total, 0, keepdims=True)
    out = out_acc[...] * share
    inner = jnp.sum(out * do_cols.astype(F32), 0, keepdims=True)

    def back_pair(p, carry):
        back_step(2 * p, 2)
        return carry

    lax.fori_loop(0, all_pairs, back_pair, 0)

    @pl.when(odd != 0)
    def _():
        back_step(2 * all_pairs, 1)

    o_ref[0] = heads_side_by_side(out).astype(BF)
    dq_ref[0] = (heads_side_by_side(dq_acc[...]) * HD ** (-0.5)).astype(BF)

    @pl.when(step == pl.num_programs(0) - 1)
    def _():
        for by, dkv_ref in enumerate(dkv_refs):
            owner = jnp.maximum(place[0] - by, 0)
            rows = pl.ds(pl.multiple_of(owner * local, 8), local)
            dkv_ref[...] = dkv_acc[rows, :].astype(BF)


def attention(place, q, do, kv, at, earlier=()):
    local = q.shape[1]
    devices = len(kv)
    keys = devices * local
    chunks = -(-keys // KEYS)
    steps = -(-local // ROWS)
    wide = H * ROWS
    by_row = pl.BlockSpec((1, ROWS, D), lambda i, p: (at, i, 0))
    pairs = pl.BlockSpec((local, 2 * HD), lambda i, p: (0, 0))
    return pl.pallas_call(
        functools.partial(attention_body, local=local, devices=devices),
        grid_spec=pltpu.PrefetchScalarGridSpec(
            num_scalar_prefetch=1,
            grid=(steps,),
            in_specs=[by_row] * 2
            + [pairs] * devices
            + [pl.BlockSpec(memory_space=pl.ANY)] * len(earlier),
            out_specs=[by_row] * 2 + [pairs] * devices,
            scratch_shapes=[
                pltpu.VMEM((chunks * KEYS, HD), BF),
                pltpu.VMEM((chunks * KEYS, HD), BF),
                pltpu.VMEM((chunks, HD, KEYS), BF),
                pltpu.VMEM((chunks, HD, KEYS), BF),
                pltpu.VMEM((chunks, KEYS, wide), F32),
                pltpu.VMEM((HD, wide), F32),
                pltpu.VMEM((HD, wide), F32),
                pltpu.VMEM((chunks * KEYS, 2 * HD), F32),
            ],
        ),
        out_shape=[jax.ShapeDtypeStruct(q.shape, BF)] * 2
        + [jax.ShapeDtypeStruct((local, 2 * HD), BF)] * devices,
        input_output_aliases={3 + devices: 0, 4 + devices: 1} if earlier else {},
        compiler_params=pltpu.CompilerParams(
            dimension_semantics=("arbitrary",), vmem_limit_bytes=VMEM_BYTES
        ),
        cost_estimate=pl.CostEstimate(
            flops=12 * local * D * keys,
            transcendentals=local * H * keys,
            bytes_accessed=8 * local * D,
        ),
    )(place, q, do, *kv, *earlier)


def feed_body(*refs, block, direct):
    h_ref, dy_ref, up_ref, down_ref, f_ref, da_ref = refs[:6]
    goal_down, goal_up = (refs[6], refs[6]) if direct else refs[6:8]
    h_cols, made_down, made_up, sem = refs[-4:]
    step, last = pl.program_id(0), pl.num_programs(0) - 1
    slot = step % 2
    width = h_ref.shape[1]

    def copies(c, at):
        if direct:
            owners, rows = made_down.shape[1], made_down.shape[2]
            part = made_up.shape[2]
            there = (
                goal_down.at[pl.ds(c * owners, owners), pl.ds(0, rows), :],
                goal_up.at[:, pl.ds(pl.multiple_of(rows + c * part, part), part), :],
            )
        else:
            span = pl.ds(pl.multiple_of(c * width, width), width)
            there = (goal_down.at[span, :], goal_up.at[:, span])
        return [
            pltpu.make_async_copy(made_down.at[at], there[0], sem.at[0, at]),
            pltpu.make_async_copy(made_up.at[at], there[1], sem.at[1, at]),
        ]

    @pl.when(step == 0)
    def _():
        h_cols[...] = h_ref[...].T

    up = up_ref[...].reshape(width, width)
    down = down_ref[...].reshape(width, width)
    for r in range(0, h_ref.shape[0], block):
        rows = pl.ds(r, block)
        pre = jnp.dot(h_ref[rows, :], up, preferred_element_type=F32)
        grad = lax.dot_general(dy_ref[rows, :], down, COLS_LAST, preferred_element_type=F32)
        below = 0.5 + 0.5 * lax.erf(pre * 0.5**0.5)
        bell = jnp.exp(pre * pre * -0.5) * (2.0 * math.pi) ** -0.5
        f_ref[rows, :] = (pre * below).astype(BF)
        da_ref[rows, :] = (grad * (below + pre * bell)).astype(BF)

    @pl.when(step >= 2)
    def _():
        for copy in copies(step - 2, slot):
            copy.wait()

    grad = lax.dot_general(f_ref[...], dy_ref[...], ROWS_FIRST, preferred_element_type=F32)
    made_down[slot] = grad.astype(BF).reshape(made_down.shape[1:])
    grad = jnp.dot(h_cols[...], da_ref[...], preferred_element_type=F32)
    made_up[slot] = grad.astype(BF).reshape(made_up.shape[1:])
    for copy in copies(step, slot):
        copy.start()

    @pl.when(step == last)
    def _():
        for copy in copies(step - 1, 1 - slot) + copies(step, slot):
            copy.wait()


def feed_weights(packed):
    owners, eight, width = packed.shape
    part = eight // 8
    if part % 16 == 0:
        return (packed, packed), (
            pl.BlockSpec((owners, part, width), lambda c: (0, 4 + c, 0)),
            pl.BlockSpec((owners // 4, 4 * part, width), lambda c: (c, 0, 0)),
        )
    down = packed[:, : 4 * part].reshape(4 * width, width)
    up = packed[:, 4 * part :].reshape(owners, 4, part, width)
    up = up.transpose(0, 2, 1, 3).reshape(width, 4 * width)
    return (up, down), (
        pl.BlockSpec((width, width), lambda c: (0, c)),
        pl.BlockSpec((width, width), lambda c: (c, 0)),
    )


def feed_forward(h, dy, weights, specs, owners):
    count, width = h.shape
    part = width // owners
    hidden = 4 * width
    direct = part % 16 == 0
    whole = pl.BlockSpec((count, width), lambda c: (0, 0))
    column = pl.BlockSpec((count, width), lambda c: (0, c))
    anywhere = pl.BlockSpec(memory_space=pl.ANY)
    if direct:
        made = [(owners // 4, 4 * part, width), (owners, part, width)]
        goals = [jax.ShapeDtypeStruct((owners, 8 * part, width), BF)]
    else:
        made = [(width, width)] * 2
        goals = [
            jax.ShapeDtypeStruct((hidden, width), BF),
            jax.ShapeDtypeStruct((width, hidden), BF),
        ]
    f, da, *grads = pl.pallas_call(
        functools.partial(feed_body, block=count // 3, direct=direct),
        grid=(4,),
        in_specs=[whole, whole, *specs],
        out_specs=[column, column] + [anywhere] * len(goals),
        out_shape=[jax.ShapeDtypeStruct((count, hidden), BF)] * 2 + goals,
        scratch_shapes=[pltpu.VMEM((width, count), BF)]
        + [pltpu.VMEM((2, *shape), BF) for shape in made]
        + [pltpu.SemaphoreType.DMA((2, 2))],
        compiler_params=pltpu.CompilerParams(
            dimension_semantics=("arbitrary",), vmem_limit_bytes=VMEM_BYTES
        ),
        cost_estimate=pl.CostEstimate(
            flops=8 * count * width * hidden,
            transcendentals=2 * count * hidden,
            bytes_accessed=4 * (count + 2 * width) * (hidden + width),
        ),
    )(h, dy, *weights)
    if direct:
        return f, da, grads[0]
    down, up = grads
    up = up.reshape(owners, part, 4, width).transpose(0, 2, 1, 3)
    packed = jnp.concatenate(
        [down.reshape(owners, 4 * part, width), up.reshape(owners, 4 * part, width)], 1
    )
    return f, da, packed


def turn(x, tables, sign=1.0):
    cosine, ahead, behind = tables
    half = ROT // 2
    return (
        x * cosine
        + pltpu.roll(x, 2 * HD - half, 1) * (sign * ahead)
        + pltpu.roll(x, half, 1) * (sign * behind)
    )


def key_only(tables):
    cosine, ahead, behind = tables
    first = lax.broadcasted_iota(jnp.int32, cosine.shape, 1) < HD
    return jnp.where(first, cosine, 1.0), jnp.where(first, ahead, 0.0), jnp.where(first, behind, 0.0)


def turn_tables(first, count):
    cosine, sine = angles(first, count)
    half = ROT // 2
    rest = jnp.zeros((count, HD - ROT), F32)
    none = jnp.zeros((count, half), F32)
    cosine = jnp.concatenate([cosine, rest + 1.0], 1)
    ahead = jnp.concatenate([-sine[:, :half], none, rest], 1)
    behind = jnp.concatenate([none, sine[:, half:], rest], 1)
    return [jnp.concatenate([t, t], 1) for t in (cosine, ahead, behind)]


def normed_rows(x):
    mean = jnp.mean(x, -1, keepdims=True)
    centered = x - mean
    scale = lax.rsqrt(jnp.mean(centered * centered, -1, keepdims=True) + EPS_NORM)
    return centered * scale, scale


def norm_rows_of(small_ref):
    return small_ref[:, pl.ds(2 * HD, 2 * HD)].astype(F32).T


def entry_body(x_ref, small_ref, cos_ref, ahead_ref, behind_ref, h1_ref, h2_ref, kv_ref, *, block):
    params = norm_rows_of(small_ref)
    weight = small_ref[:, pl.ds(0, 2 * HD)]
    for r in range(0, x_ref.shape[1], block):
        rows = pl.ds(r, block)
        normed, _ = normed_rows(x_ref[0, rows, :].astype(F32))
        first = (normed * params[0:1] + params[1:2]).astype(BF)
        h1_ref[0, rows, :] = first
        h2_ref[0, rows, :] = (normed * params[2:3] + params[3:4]).astype(BF)
        pair = jnp.dot(first, weight, preferred_element_type=F32)
        tables = key_only([t[rows, :] for t in (cos_ref, ahead_ref, behind_ref)])
        kv_ref[0, rows, :] = turn(pair, tables).astype(BF)


def entry(x, small, tables):
    batch, local, width = x.shape
    rows = pl.BlockSpec((1, local, width), lambda b: (b, 0, 0))
    table = pl.BlockSpec((local, 2 * HD), lambda b: (0, 0))
    return pl.pallas_call(
        functools.partial(entry_body, block=local // 3),
        grid=(batch,),
        in_specs=[rows, pl.BlockSpec(small.shape, lambda b: (0, 0)), table, table, table],
        out_specs=[rows, rows, pl.BlockSpec((1, local, 2 * HD), lambda b: (b, 0, 0))],
        out_shape=[jax.ShapeDtypeStruct(x.shape, BF)] * 2
        + [jax.ShapeDtypeStruct((batch, local, 2 * HD), BF)],
        compiler_params=pltpu.CompilerParams(
            dimension_semantics=("arbitrary",), vmem_limit_bytes=VMEM_BYTES
        ),
        cost_estimate=pl.CostEstimate(
            flops=4 * batch * local * width * HD,
            transcendentals=batch * local,
            bytes_accessed=8 * batch * local * width,
        ),
    )(x, small, *tables)


def query_body(h_ref, dy_ref, weight_ref, cos_ref, ahead_ref, behind_ref, q_ref, do_ref):
    mixed = jnp.dot(h_ref[0], weight_ref[:, pl.ds(0, D)], preferred_element_type=F32)
    tables = cos_ref[...], ahead_ref[...], behind_ref[...]
    for c in range(0, D, 2 * HD):
        q = turn(mixed[:, c : c + 2 * HD], tables).astype(BF)
        q_ref[0, :, pl.ds(c, 2 * HD)] = q * BF(HD ** (-0.5))
    do_ref[0] = lax.dot_general(
        dy_ref[0], weight_ref[:, pl.ds(D, D)], COLS_LAST, preferred_element_type=F32
    ).astype(BF)


def queries(h, dy, middle, tables):
    batch, local, width = h.shape
    rows = pl.BlockSpec((1, local, width), lambda b: (b, 0, 0))
    table = pl.BlockSpec((local, 2 * HD), lambda b: (0, 0))
    return pl.pallas_call(
        query_body,
        grid=(batch,),
        in_specs=[rows, rows, pl.BlockSpec(middle.shape, lambda b: (0, 0)), table, table, table],
        out_specs=[rows, rows],
        out_shape=[jax.ShapeDtypeStruct(h.shape, BF)] * 2,
        compiler_params=pltpu.CompilerParams(
            dimension_semantics=("arbitrary",), vmem_limit_bytes=VMEM_BYTES
        ),
        cost_estimate=pl.CostEstimate(
            flops=4 * batch * local * width * width,
            transcendentals=0,
            bytes_accessed=8 * batch * local * width,
        ),
    )(h, dy, middle, *tables)


def back_body(
    core_of, weight_of, x_ref, cot_ref, h_ref, o_ref, dq_ref, dh2_ref, middle_ref, small_ref,
    cos_ref, ahead_ref, behind_ref, *refs, devices,
):
    pair_refs, refs = refs[: devices * weight_of.shape[0]], refs[devices * weight_of.shape[0] :]
    dx_ref, *grad_refs, acc, norm_acc, pair_acc = refs
    b, last = pl.program_id(0), pl.num_programs(0) - 1
    tables = cos_ref[...], ahead_ref[...], behind_ref[...]
    params = norm_rows_of(small_ref)
    dy = cot_ref[0].astype(F32) * weight_of[b]
    dy_low = dy.astype(BF)
    for at in range(weight_of.shape[0]):

        @pl.when(b == at)
        def _(parts=pair_refs[devices * at : devices * (at + 1)]):
            total = parts[0][...].astype(F32)
            for part in parts[1:]:
                total = total + part[...].astype(F32)
            pair_acc[...] = total.astype(BF).astype(F32)

    pair = turn(pair_acc[...], key_only(tables), -1.0).astype(BF)
    turned = [
        turn(dq_ref[0, :, pl.ds(c, 2 * HD)].astype(F32), tables, -1.0).astype(BF)
        for c in range(0, D, 2 * HD)
    ]
    dz = jnp.concatenate(turned + [pair], 1)
    wide = dz.shape[1]
    made = lax.dot_general(h_ref[0], dz, ROWS_FIRST, preferred_element_type=F32)
    made_out = lax.dot_general(o_ref[0], dy_low, ROWS_FIRST, preferred_element_type=F32)

    @pl.when(b == 0)
    def _():
        acc[:, pl.ds(0, wide)] = made
        acc[:, pl.ds(wide, D)] = made_out
        norm_acc[...] = jnp.zeros_like(norm_acc)

    @pl.when(b > 0)
    def _():
        acc[:, pl.ds(0, wide)] += made
        acc[:, pl.ds(wide, D)] += made_out

    weights = jnp.concatenate([middle_ref[:, pl.ds(0, D)], small_ref[:, pl.ds(0, 2 * HD)]], 1)
    dh1 = lax.dot_general(dz, weights, COLS_LAST, preferred_element_type=F32)
    dh2 = dh2_ref[0]
    normed, scale = normed_rows(x_ref[0].astype(F32))
    norm_acc[0:1] += jnp.sum(dh1 * normed, 0, keepdims=True)
    norm_acc[1:2] += jnp.sum(dh1, 0, keepdims=True)
    norm_acc[2:3] += jnp.sum(dh2 * normed, 0, keepdims=True)
    norm_acc[3:4] += jnp.sum(dh2, 0, keepdims=True)
    inner = dh1 * params[0:1] + dh2 * params[2:3]
    inner = inner - jnp.mean(inner, -1, keepdims=True) - normed * jnp.mean(
        inner * normed, -1, keepdims=True
    )
    dx_ref[0] = (dy + scale * inner).astype(BF)

    @pl.when(b == last)
    def _():
        acc[:, pl.ds(wide + D, 2 * HD)] = norm_acc[...].T
        if len(grad_refs) == 1:
            grad_refs[0][...] = acc[...].astype(BF)
            return
        send_ref, keep_ref = grad_refs
        pairs, part, _ = send_ref.shape
        for p in range(pairs):
            for ref, core in ((send_ref, 1 - core_of[0]), (keep_ref, core_of[0])):
                rows = pl.ds(pl.multiple_of((2 * p + core) * part, part), part)
                ref[p] = acc[rows, :].astype(ref.dtype)


def back(core, row_weight, owners, x, cot, h, o, dq, pairs, dh2, middle, small, tables):
    batch, local, width = x.shape
    rows = pl.BlockSpec((1, local, width), lambda b, *s: (b, 0, 0))
    table = pl.BlockSpec((local, 2 * HD), lambda b, *s: (0, 0))
    columns = 2 * width + 4 * HD
    part = width // owners
    if part % 16 == 0:
        half = (owners // 2, part, columns)
        made = [jax.ShapeDtypeStruct(half, BF), jax.ShapeDtypeStruct(half, F32)]
    else:
        made = [jax.ShapeDtypeStruct((width, columns), BF)]
    return pl.pallas_call(
        functools.partial(back_body, devices=len(pairs[0])),
        grid_spec=pltpu.PrefetchScalarGridSpec(
            num_scalar_prefetch=2,
            grid=(batch,),
            in_specs=[rows] * 6
            + [pl.BlockSpec(w.shape, lambda b, *s: (0, 0)) for w in (middle, small)]
            + [table] * (3 + sum(len(parts) for parts in pairs)),
            out_specs=[rows]
            + [pl.BlockSpec(m.shape, lambda b, *s, n=len(m.shape): (0,) * n) for m in made],
            scratch_shapes=[
                pltpu.VMEM((width, columns), F32),
                pltpu.VMEM((2 * HD, width), F32),
                pltpu.VMEM((local, 2 * HD), F32),
            ],
        ),
        out_shape=[jax.ShapeDtypeStruct(x.shape, BF), *made],
        compiler_params=pltpu.CompilerParams(
            dimension_semantics=("arbitrary",), vmem_limit_bytes=VMEM_BYTES
        ),
        cost_estimate=pl.CostEstimate(
            flops=6 * batch * local * width * width,
            transcendentals=batch * local,
            bytes_accessed=16 * batch * local * width,
        ),
    )(
        core, row_weight, x, cot, h, o, dq, dh2, middle, small, *tables,
        *[part for parts in pairs for part in parts],
    )


def sum_body(a_ref, w_ref, out_ref):
    width = out_ref.shape[1]
    part = lax.dot_general(
        a_ref[...], w_ref[...].reshape(width, width), COLS_LAST, preferred_element_type=F32
    )

    @pl.when(pl.program_id(0) == 0)
    def _():
        out_ref[...] = part

    @pl.when(pl.program_id(0) > 0)
    def _():
        out_ref[...] += part


def up_back(da, weights, specs):
    count, hidden = da.shape
    width = hidden // 4
    return pl.pallas_call(
        sum_body,
        grid=(4,),
        in_specs=[pl.BlockSpec((count, width), lambda c: (0, c)), specs[0]],
        out_specs=pl.BlockSpec((count, width), lambda c: (0, 0)),
        out_shape=jax.ShapeDtypeStruct((count, width), F32),
        compiler_params=pltpu.CompilerParams(
            dimension_semantics=("arbitrary",), vmem_limit_bytes=VMEM_BYTES
        ),
        cost_estimate=pl.CostEstimate(
            flops=2 * count * width * hidden,
            transcendentals=0,
            bytes_accessed=2 * count * hidden + 4 * count * width + 2 * width * hidden,
        ),
    )(da, weights[0])


def output_body(x_ref, o_ref, out_w_ref, f_ref, w_ref, y_ref, acc):
    step, last = pl.program_id(0), pl.num_programs(0) - 1
    width = acc.shape[1]
    part = jnp.dot(f_ref[...], w_ref[...].reshape(width, width), preferred_element_type=F32)

    @pl.when(step == 0)
    def _():
        heads = jnp.dot(o_ref[...], out_w_ref[...], preferred_element_type=F32)
        acc[...] = x_ref[...].astype(F32) + heads + part

    @pl.when(step > 0)
    def _():
        acc[...] += part

    @pl.when(step == last)
    def _():
        y_ref[...] = acc[...].astype(BF)


def output(x, o, middle, f, weights, specs):
    count, hidden = f.shape
    width = hidden // 4
    whole = pl.BlockSpec((count, width), lambda c: (0, 0))
    return pl.pallas_call(
        output_body,
        grid=(4,),
        in_specs=[
            whole,
            whole,
            pl.BlockSpec((width, width), lambda c: (0, 1)),
            pl.BlockSpec((count, width), lambda c: (0, c)),
            specs[1],
        ],
        out_specs=whole,
        out_shape=jax.ShapeDtypeStruct((count, width), BF),
        scratch_shapes=[pltpu.VMEM((count, width), F32)],
        compiler_params=pltpu.CompilerParams(
            dimension_semantics=("arbitrary",), vmem_limit_bytes=VMEM_BYTES
        ),
        cost_estimate=pl.CostEstimate(
            flops=2 * count * width * (hidden + width),
            transcendentals=0,
            bytes_accessed=2 * (count + width) * hidden + 6 * count * width,
        ),
    )(x, o, middle, f, weights[1])


def adam_store(weight_ref, first_ref, second_ref, grad, outs, rate, decay):
    results = adam_update(weight_ref[...], first_ref[...], second_ref[...], grad, rate, decay)
    for out_ref, result in zip(outs, results):
        out_ref[...] = result


def adam_body(seq_at, factor_ref, up_grad_ref, down_grad_ref, *refs):
    parts, refs, joined = refs[:4], refs[4:-1], refs[-1]
    factor = factor_ref[0, 0]
    qkv, out, up, down, norm = [refs[3 * i : 3 * i + 3] for i in range(5)]
    outs = refs[15:]
    qkv_out, out_out, up_out, down_out, norm_out = [outs[3 * i : 3 * i + 3] for i in range(5)]
    adam_store(*up, up_grad_ref[...].astype(F32) * factor, up_out, RATE_SMALL, DECAY)
    adam_store(*down, down_grad_ref[...].astype(F32) * factor, down_out, RATE_SMALL, DECAY)

    @pl.when(pl.program_id(0) == pl.num_programs(0) - 1)
    def _():
        for mask, ref in enumerate(parts):
            joined[seq_at[0] ^ mask] = unpack_quarter(ref)
        rest = joined[...].reshape(-1, joined.shape[2])
        wide = qkv[0].shape[1]
        adam_store(*qkv, rest[:, :wide] * factor, qkv_out, RATE_SMALL, DECAY)
        adam_store(*out, rest[:, wide : wide + D] * factor, out_out, RATE_LARGE, DECAY)
        grad = rest[:, wide + D :].T[:4] * factor
        adam_store(*norm, grad, norm_out, RATE_NORM, 0.0)


def adam_all(seq_at, factor, feed, rest, qkv, out, up, down, norm):
    part, hidden = up[0].shape
    width = hidden // 4
    column = pl.BlockSpec((part, width), lambda c, p: (0, c))
    row = pl.BlockSpec((part, width), lambda c, p: (c, 0))

    def whole(x):
        return pl.BlockSpec(x.shape, lambda c, p: (0, 0))

    states = [*qkv, *out, *up, *down, *norm]
    specs = (
        [whole(x) for x in qkv + out] + [column] * 3 + [row] * 3 + [whole(x) for x in norm]
    )
    return pl.pallas_call(
        adam_body,
        grid_spec=pltpu.PrefetchScalarGridSpec(
            num_scalar_prefetch=1,
            grid=(4,),
            in_specs=[
                pl.BlockSpec(memory_space=pltpu.SMEM),
                pl.BlockSpec((part, width), lambda c, p: (4 + c, 0)),
                row,
                *[whole(x) for x in rest],
                *specs,
            ],
            out_specs=specs,
            scratch_shapes=[pltpu.VMEM((4, rest[0].shape[0], rest[0].shape[1] - 2 * HD), F32)],
        ),
        out_shape=[jax.ShapeDtypeStruct(x.shape, F32) for x in states],
        compiler_params=pltpu.CompilerParams(
            dimension_semantics=("arbitrary",), vmem_limit_bytes=VMEM_BYTES
        ),
    )(seq_at, factor, feed, feed, *rest, *states)


def swap(x, axis, mask):
    return lax.ppermute(x, axis, [(i, i ^ mask) for i in range(lax.axis_size(axis))])


def local_call(body, at, inputs, shapes, scratch=()):
    return pl.pallas_call(
        body,
        grid_spec=pltpu.PrefetchScalarGridSpec(
            num_scalar_prefetch=1,
            grid=(1,),
            in_specs=[pl.BlockSpec(a.shape, lambda i, p, n=a.ndim: (0,) * n) for a in inputs],
            out_specs=[pl.BlockSpec(s, lambda i, p, n=len(s): (0,) * n) for s, _ in shapes],
            scratch_shapes=list(scratch),
        ),
        out_shape=[jax.ShapeDtypeStruct(s, kind) for s, kind in shapes],
        compiler_params=pltpu.CompilerParams(
            dimension_semantics=("arbitrary",), vmem_limit_bytes=VMEM_BYTES // 3
        ),
    )(at, *inputs)


def split_chips(at, keep, came, send_left, send_right, keep_left, keep_right):
    x, y = at[0], at[1]
    half = send_left.shape[2]
    left, right = pl.ds(0, half), pl.ds(half, half)
    for i in range(2):
        for ref, block, columns in (
            (send_left, 2 * i + 1 - x, left),
            (keep_left, 2 * i + x, left),
            (send_right, 2 * (1 - y) + i, right),
            (keep_right, 2 * y + i, right),
        ):
            total = keep[block, :, columns] + came[block, :, columns].astype(F32)
            ref[i] = total.astype(ref.dtype)


def split_last(at, left, right, a, b, send_left, send_right, keep_left, keep_right):
    x, y = at[0], at[1]
    for ref, keep, came, block in (
        (send_left, left, a, 1 - y),
        (keep_left, left, a, y),
        (send_right, right, b, 1 - x),
        (keep_right, right, b, x),
    ):
        ref[...] = (keep[block] + came[block].astype(F32)).astype(ref.dtype)


def split_seq(at, left, right, a, b, one, two, three, keep, total):
    half = left.shape[1]
    quarters, rows, _ = total.shape
    total[:, :, pl.ds(0, half)] = (left[...] + a[...].astype(F32)).reshape(quarters, rows, half)
    total[:, :, pl.ds(half, half)] = (right[...] + b[...].astype(F32)).reshape(quarters, rows, half)
    seq = at[2]
    keep[...] = total[seq]
    for mask, ref in ((1, one), (2, two), (3, three)):
        ref[...] = total[seq ^ mask].astype(BF)


def pack_quarter(at, keep, one, two, three, packed):
    total = keep[...]
    for ref in (one, two, three):
        total = total + ref[...].astype(F32)
    wide = total.shape[1]
    packed[:, pl.ds(0, wide)] = total.astype(BF)
    pair = total[:, D : D + 2 * HD]
    packed[:, pl.ds(wide, 2 * HD)] = (pair - pair.astype(BF).astype(F32)).astype(BF)


def unpack_quarter(ref):
    wide = ref.shape[1] - 2 * HD
    pair = pl.ds(D, 2 * HD)
    after = D + 2 * HD
    return jnp.concatenate(
        [
            ref[:, pl.ds(0, D)].astype(F32),
            ref[:, pair].astype(F32) + ref[:, pl.ds(wide, 2 * HD)].astype(F32),
            ref[:, pl.ds(after, wide - after)].astype(F32),
        ],
        1,
    )


def add_squares(at, *refs):
    *quarters, feed, squares = refs
    total = jnp.zeros(squares.shape, F32)
    for grad in [unpack_quarter(ref) for ref in quarters] + [feed[...].astype(F32)]:
        parts = jnp.sum(jnp.square(grad), 0, keepdims=True)
        for c in range(0, grad.shape[1], 2 * HD):
            total = total + parts[:, c : c + 2 * HD]
    squares[...] = total


def beside(sends, work=lambda: (), inputs=()):
    flat, inputs = lax.optimization_barrier(([x for x, _, _ in sends], inputs))
    came = [swap(x, axis, mask) for x, (_, axis, mask) in zip(flat, sends)]
    return lax.optimization_barrier((came, work(*inputs)))


def batch_sum(at, send, keep, work, inputs):
    (came,), _ = beside([(send, "batch", 1)])
    _, r, c = keep.shape
    two, one, quarter = (2, r, c // 2), (r, c // 2), (r // 4, c)
    send_left, send_right, left, right = local_call(
        split_chips, at, [keep, came], [(two, BF), (two, BF), (two, F32), (two, F32)]
    )
    (a, b), _ = beside([(send_left, "batch", 2), (send_right, "batch", 4)])
    send_left, send_right, left, right = local_call(
        split_last, at, [left, right, a, b], [(one, BF), (one, BF), (one, F32), (one, F32)]
    )
    (a, b), _ = beside([(send_left, "batch", 4), (send_right, "batch", 2)])
    *sends, keep = local_call(
        split_seq,
        at,
        [left, right, a, b],
        [(quarter, BF)] * 3 + [(quarter, F32)],
        [pltpu.VMEM((4, *quarter), F32)],
    )
    came, result = beside([(x, "seq", m + 1) for m, x in enumerate(sends)], work, inputs)
    (own,) = local_call(pack_quarter, at, [keep, *came], [((r // 4, c + 2 * HD), BF)])
    came, _ = beside([(own, "seq", mask) for mask in (1, 2, 3)])
    return [own, *came], result


def shift(x, by):
    count = lax.axis_size("seq")
    return lax.ppermute(x, "seq", [(s, s + by) for s in range(count) if 0 <= s + by < count])


def shards(
    tokens,
    cotangent,
    tags,
    loss_weights,
    w_qkv,
    m_qkv,
    v_qkv,
    w_out,
    m_out,
    v_out,
    w_up,
    m_up,
    v_up,
    w_down,
    m_down,
    v_down,
    norm_params,
    m_norm,
    v_norm,
):
    owners = lax.axis_size("batch")
    seq_count = lax.axis_size("seq")
    seq_at = lax.axis_index("seq")
    seq_rows, local, width = tokens.shape
    count = seq_rows * local
    part = w_qkv.shape[0]
    fence = lax.optimization_barrier

    small = jnp.concatenate(
        [w_qkv[:, D:], norm_params.T, jnp.zeros((part, 2 * HD - 4), F32)], 1
    ).astype(BF)
    small = lax.all_gather(small, "batch", axis=0, tiled=True)
    middle = jnp.concatenate([w_qkv[:, :D], w_out], 1).astype(BF)
    middle = lax.all_gather(middle, "batch", axis=0, tiled=True)
    packed = jnp.concatenate([w_down] + [w_up[:, D * i : D * (i + 1)] for i in range(4)], 0)
    packed, small = fence((packed.astype(BF), small))
    packed = lax.all_gather(packed, "batch", axis=0, tiled=True).reshape(owners, 8 * part, D)
    weights, specs = feed_weights(packed)

    tables = turn_tables(seq_at * local, local)
    subsets = jnp.arange(loss_weights.shape[0])
    row_weight = jnp.sum(
        jnp.where(tags[:, None] == subsets[None, :], loss_weights[None, :], 0.0), -1
    )
    grad_low = (cotangent.astype(F32) * row_weight[:, None, None]).astype(BF)

    first_low, second_low, pair = entry(tokens, small, tables)
    query, grad_heads = queries(first_low, grad_low, middle, tables)

    def gather_pair(own):
        return [own] + [shift(own, by) for by in range(1, seq_count)]

    arrived, query = fence((gather_pair(pair[0]), query))
    place = jnp.reshape(seq_at, (1,)).astype(jnp.int32)

    state, came = (), []
    for at in range(seq_rows):
        if at == seq_rows // 2:
            second_low, state = fence((second_low, state))
            active_low, grad_up_pre, grad_feed = feed_forward(
                second_low.reshape(count, D), grad_low.reshape(count, D), weights, specs, owners
            )
            feed_sum = lax.psum_scatter(
                grad_feed.reshape(owners * 8 * part, D), "batch", scatter_dimension=0, tiled=True
            )
            state, grad_up_pre = fence((state, grad_up_pre))
        keys = arrived
        if at + 1 < seq_rows:
            own, keys = fence((pair[at + 1], keys))
            arrived = gather_pair(own)
        heads, grad_query, *grad_pair = attention(place, query, grad_heads, keys, at, state)
        state = heads, grad_query
        came.append([shift(g, -by) if by else g for by, g in enumerate(grad_pair)])
        if at + 1 < seq_rows:
            arrived, state = fence((arrived, state))
    heads, grad_query = state

    grad_up_pre, heads = fence((grad_up_pre, heads))
    grad_second = up_back(grad_up_pre, weights, specs)
    came, grad_second, feed_sum = fence((came, grad_second, feed_sum))
    feed_sum = lax.psum(feed_sum, "seq")

    def input_side():
        return back(
            jnp.reshape(lax.axis_index("batch") % 2, (1,)),
            row_weight,
            owners,
            tokens,
            cotangent,
            first_low,
            heads,
            grad_query,
            came,
            grad_second.reshape(seq_rows, local, D),
            middle,
            small,
            tables,
        )

    def output_side(x, o, w, f):
        return output(x, o, w, f, weights, specs)

    output_inputs = tokens.reshape(count, D), heads.reshape(count, D), middle, active_low

    if owners == 8 and seq_count == 4:
        batch_at = lax.axis_index("batch")
        at = jnp.stack([(batch_at // 2) % 2, batch_at // 4, seq_at])

        def rest_of_layer(_, carry):
            input_grad, send, keep = input_side()
            parts, layer_out = batch_sum(at, send, keep, output_side, output_inputs)
            return input_grad, layer_out, parts

        quarter = (part // 4, w_qkv.shape[1] + D + 4 * HD)
        unused = (
            second_low,
            query.reshape(count, D),
            [jnp.zeros(quarter, BF)] * 4,
        )
        once = 1 + jnp.minimum(tags[0], 0)
        input_grad, layer_out, rest = lax.fori_loop(0, once, rest_of_layer, unused)
        feed_sum, rest = fence((feed_sum, rest))
        (squares,) = local_call(add_squares, at, [*rest, feed_sum], [((1, 2 * HD), F32)])
        total_squares = lax.psum(jnp.sum(squares), "batch")
    else:
        input_grad, rest = input_side()
        layer_out = output_side(*output_inputs)
        rest = lax.psum_scatter(rest.astype(F32), "batch", scatter_dimension=0, tiled=True)
        rest = lax.psum(rest, "seq")
        squares = [jnp.sum(jnp.square(x.astype(F32))) for x in (rest, feed_sum)]
        total_squares = lax.psum(sum(squares), "batch")
    layer_out = layer_out.reshape(seq_rows, local, D)
    grad_norm = jnp.sqrt(total_squares)
    factor = CLIP_NORM / jnp.maximum(grad_norm, CLIP_NORM)
    states = (
        (w_qkv, m_qkv, v_qkv),
        (w_out, m_out, v_out),
        (w_up, m_up, v_up),
        (w_down, m_down, v_down),
        (norm_params, m_norm, v_norm),
    )
    if isinstance(rest, list):
        results = adam_all(at[2:], factor.reshape(1, 1), feed_sum, rest, *states)
    else:
        qkv_width = w_qkv.shape[1]
        down_sum, up_sum = feed_sum[: 4 * part], feed_sum[4 * part :]
        up_sum = up_sum.astype(F32).reshape(4, part, D).transpose(1, 0, 2)
        grads = (
            rest[:, :qkv_width],
            rest[:, qkv_width : qkv_width + D],
            up_sum.reshape(part, 4 * D),
            down_sum.astype(F32),
            rest[:, qkv_width + D : qkv_width + D + 4].T,
        )
        rates = (RATE_SMALL, RATE_LARGE, RATE_SMALL, RATE_SMALL, RATE_NORM)
        decays = (DECAY, DECAY, DECAY, DECAY, 0.0)
        results = []
        for three, grad, rate, decay in zip(states, grads, rates, decays):
            results.extend(adam_update(*three, grad * factor, rate, decay))
    return (layer_out, input_grad, grad_norm, *results)


def solution(mesh):
    in_specs = (
        P("batch", "seq", None),
        P("batch", "seq", None),
        P("batch"),
        P(),
        P("batch", None),
        P("batch", None),
        P("batch", None),
        P("batch", None),
        P("batch", None),
        P("batch", None),
        P("batch", None),
        P("batch", None),
        P("batch", None),
        P("batch", None),
        P("batch", None),
        P("batch", None),
        P(None, "batch"),
        P(None, "batch"),
        P(None, "batch"),
    )
    out_specs = (
        P("batch", "seq", None),
        P("batch", "seq", None),
        P(),
        P("batch", None),
        P("batch", None),
        P("batch", None),
        P("batch", None),
        P("batch", None),
        P("batch", None),
        P("batch", None),
        P("batch", None),
        P("batch", None),
        P("batch", None),
        P("batch", None),
        P("batch", None),
        P(None, "batch"),
        P(None, "batch"),
        P(None, "batch"),
    )
    return jax.shard_map(shards, mesh=mesh, in_specs=in_specs, out_specs=out_specs, check_vma=False)
```

```python
import functools
import math

import jax
import jax.numpy as jnp
from jax import lax
from jax.experimental import pallas as pl
from jax.experimental.pallas import tpu as pltpu
from jax.sharding import PartitionSpec as P

D = 768
H = 12
HD = 64
ROT = 16
STEP = 10


EPS_NORM = 1e-05
BETA_ONE = 0.9
BETA_TWO = 0.999
ADAM_EPS = 1e-08
CLIP_NORM = 1.0
RATE_SMALL = 0.02
RATE_LARGE = 0.2
RATE_NORM = 1.0
DECAY = 0.1
ROWS_FIRST = (((0,), (0,)), ((), ()))
COLS_LAST = (((1,), (1,)), ((), ()))


def angles(first, count):
    place = (first + jnp.arange(count)).astype(jnp.float32)
    inverse = 10000.0 ** (-jnp.arange(0, ROT, 2).astype(jnp.float32) / ROT)
    turn = place[:, None] * inverse[None, :]
    turn = jnp.concatenate([turn, turn], -1)
    return (jnp.cos(turn), jnp.sin(turn))


def adam_update(weight, first, second, grad, rate, decay):
    first_new = BETA_ONE * first + (1.0 - BETA_ONE) * grad
    second_new = BETA_TWO * second + (1.0 - BETA_TWO) * grad * grad
    step_one = first_new / (1.0 - BETA_ONE**STEP)
    step_two = second_new / (1.0 - BETA_TWO**STEP)
    weight_new = weight - rate * (step_one / (jnp.sqrt(step_two) + ADAM_EPS) + decay * weight)
    return (weight_new, first_new, second_new)


BF = jnp.bfloat16
F32 = jnp.float32
ROWS = 128
KEYS = 384
VMEM_BYTES = 60 << 20


def attention_body(
    place,
    q_ref,
    do_ref,
    *refs,
    local,
    devices,
):
    kv_refs, refs = refs[:devices], refs[-10 - devices :]
    o_ref, dq_ref, dkv_refs = refs[0], refs[1], refs[2 : 2 + devices]
    k_rows, v_rows, k_cols, v_cols, scores, out_acc, dq_acc, dkv_acc = refs[-8:]
    step = pl.program_id(0)
    chunks = scores.shape[0]
    wide = H * ROWS

    @pl.when(step == 0)
    def _():
        dkv_acc[...] = jnp.zeros_like(dkv_acc)
        for by, kv_ref in enumerate(kv_refs):

            @pl.when(place[0] >= by)
            def _(by=by, kv_ref=kv_ref):
                rows = pl.ds(pl.multiple_of((place[0] - by) * local, 8), local)
                dkv_acc[rows, :] = kv_ref[...].astype(F32)

        def prepare(j, carry):
            rows = pl.ds(pl.multiple_of(j * KEYS, KEYS), KEYS)
            pair = dkv_acc[rows, :].astype(BF)
            k_rows[rows, :] = pair[:, :HD]
            v_rows[rows, :] = pair[:, HD:]
            turned = pair.T
            k_cols[j] = turned[:HD]
            v_cols[j] = turned[HD:]
            dkv_acc[rows, :] = jnp.zeros((KEYS, 2 * HD), F32)
            return carry

        lax.fori_loop(0, chunks, prepare, 0)

    start = place[0] * local + step * ROWS
    last = jnp.minimum(start + ROWS - 1, (place[0] + 1) * local - 1)
    open_chunks = (start + 1) // KEYS
    all_chunks = last // KEYS + 1

    def heads_in_columns(x):
        turned = [x[:, 2 * HD * p : 2 * HD * (p + 1)].T for p in range(H // 2)]
        return jnp.concatenate([t[a : a + HD] for t in turned for a in (0, HD)], 1)

    def heads_in_rows(x):
        return jnp.concatenate([x[:, HD * h : HD * (h + 1)] for h in range(H)], 0)

    def heads_side_by_side(t):
        return jnp.concatenate(
            [
                jnp.concatenate(
                    [
                        t[:, 2 * p * ROWS : (2 * p + 1) * ROWS],
                        t[:, (2 * p + 1) * ROWS : (2 * p + 2) * ROWS],
                    ],
                    0,
                ).T
                for p in range(H // 2)
            ],
            1,
        )

    real = lax.broadcasted_iota(jnp.int32, (ROWS, D), 0) < local - step * ROWS
    q = jnp.where(real, q_ref[0], 0.0).astype(BF)
    do = jnp.where(real, do_ref[0], 0.0).astype(BF)
    q_cols = heads_in_columns(q)
    do_cols = heads_in_columns(do)
    blank = jnp.zeros((wide, HD), BF)
    q_side = jnp.concatenate([heads_in_rows(q), blank], 1)
    do_side = jnp.concatenate([blank, heads_in_rows(do)], 1)
    out_acc[...] = jnp.zeros_like(out_acc)
    dq_acc[...] = jnp.zeros_like(dq_acc)
    lane = lax.broadcasted_iota(jnp.int32, (1, wide), 1)
    query_at = start + (lane & (ROWS - 1))

    open_pairs, all_pairs, odd = open_chunks // 2, all_chunks // 2, all_chunks % 2

    def key_rows(j, count):
        return pl.ds(pl.multiple_of(j * KEYS, KEYS), count * KEYS)

    def columns(ref, j, count):
        return jnp.concatenate([ref[j + c] for c in range(count)], 1)

    def score_step(j, top, count, masked):
        raw = jnp.dot(k_rows[key_rows(j, count), :], q_cols, preferred_element_type=F32)
        if masked:
            key_at = j * KEYS + lax.broadcasted_iota(jnp.int32, (count * KEYS, wide), 0)
            raw = jnp.where(key_at <= query_at, raw, -1e30)
        scores[pl.ds(j, count)] = raw.reshape(count, KEYS, wide)
        return jnp.maximum(top, jnp.max(raw.reshape(count * KEYS // 8, 8, wide), 0))

    def value_step(j, total, count):
        expo = jnp.exp(scores[pl.ds(j, count)].reshape(count * KEYS, wide) - top)
        scores[pl.ds(j, count)] = expo.reshape(count, KEYS, wide)
        out_acc[...] += jnp.dot(
            columns(v_cols, j, count), expo.astype(BF), preferred_element_type=F32
        )
        return total + jnp.sum(expo.reshape(count * KEYS // 8, 8, wide), 0)

    def back_step(j, count):
        rows = key_rows(j, count)
        grad_probs = jnp.dot(v_rows[rows, :], do_cols, preferred_element_type=F32)
        probs = scores[pl.ds(j, count)].reshape(count * KEYS, wide) * share
        grad_scores = (probs * (grad_probs - inner)).astype(BF)
        dkv_acc[rows, :] += jnp.dot(
            grad_scores, q_side, preferred_element_type=F32
        ) + jnp.dot(probs.astype(BF), do_side, preferred_element_type=F32)
        dq_acc[...] += jnp.dot(
            columns(k_cols, j, count), grad_scores, preferred_element_type=F32
        )

    top = jnp.full((8, wide), -1e30, F32)
    top = lax.fori_loop(0, open_pairs, lambda p, t: score_step(2 * p, t, 2, False), top)
    top = lax.fori_loop(open_pairs, all_pairs, lambda p, t: score_step(2 * p, t, 2, True), top)
    top = lax.fori_loop(0, odd, lambda p, t: score_step(2 * all_pairs, t, 1, True), top)
    top = jnp.max(top, 0, keepdims=True)

    total = jnp.zeros((8, wide), F32)
    total = lax.fori_loop(0, all_pairs, lambda p, t: value_step(2 * p, t, 2), total)
    total = lax.fori_loop(0, odd, lambda p, t: value_step(2 * all_pairs, t, 1), total)
    share = 1.0 / jnp.sum(total, 0, keepdims=True)
    out = out_acc[...] * share
    inner = jnp.sum(out * do_cols.astype(F32), 0, keepdims=True)

    def back_pair(p, carry):
        back_step(2 * p, 2)
        return carry

    lax.fori_loop(0, all_pairs, back_pair, 0)

    @pl.when(odd != 0)
    def _():
        back_step(2 * all_pairs, 1)

    o_ref[0] = heads_side_by_side(out).astype(BF)
    dq_ref[0] = (heads_side_by_side(dq_acc[...]) * HD ** (-0.5)).astype(BF)

    @pl.when(step == pl.num_programs(0) - 1)
    def _():
        for by, dkv_ref in enumerate(dkv_refs):
            owner = jnp.maximum(place[0] - by, 0)
            rows = pl.ds(pl.multiple_of(owner * local, 8), local)
            dkv_ref[...] = dkv_acc[rows, :].astype(BF)


def attention(place, q, do, kv, at, earlier=()):
    local = q.shape[1]
    devices = len(kv)
    keys = devices * local
    chunks = -(-keys // KEYS)
    steps = -(-local // ROWS)
    wide = H * ROWS
    by_row = pl.BlockSpec((1, ROWS, D), lambda i, p: (at, i, 0))
    pairs = pl.BlockSpec((local, 2 * HD), lambda i, p: (0, 0))
    return pl.pallas_call(
        functools.partial(attention_body, local=local, devices=devices),
        grid_spec=pltpu.PrefetchScalarGridSpec(
            num_scalar_prefetch=1,
            grid=(steps,),
            in_specs=[by_row] * 2
            + [pairs] * devices
            + [pl.BlockSpec(memory_space=pl.ANY)] * len(earlier),
            out_specs=[by_row] * 2 + [pairs] * devices,
            scratch_shapes=[
                pltpu.VMEM((chunks * KEYS, HD), BF),
                pltpu.VMEM((chunks * KEYS, HD), BF),
                pltpu.VMEM((chunks, HD, KEYS), BF),
                pltpu.VMEM((chunks, HD, KEYS), BF),
                pltpu.VMEM((chunks, KEYS, wide), F32),
                pltpu.VMEM((HD, wide), F32),
                pltpu.VMEM((HD, wide), F32),
                pltpu.VMEM((chunks * KEYS, 2 * HD), F32),
            ],
        ),
        out_shape=[jax.ShapeDtypeStruct(q.shape, BF)] * 2
        + [jax.ShapeDtypeStruct((local, 2 * HD), BF)] * devices,
        input_output_aliases={3 + devices: 0, 4 + devices: 1} if earlier else {},
        compiler_params=pltpu.CompilerParams(
            dimension_semantics=("arbitrary",), vmem_limit_bytes=VMEM_BYTES
        ),
        cost_estimate=pl.CostEstimate(
            flops=12 * local * D * keys,
            transcendentals=local * H * keys,
            bytes_accessed=8 * local * D,
        ),
    )(place, q, do, *kv, *earlier)


def feed_body(*refs, block, direct):
    h_ref, dy_ref, up_ref, down_ref, f_ref, da_ref = refs[:6]
    goal_down, goal_up = (refs[6], refs[6]) if direct else refs[6:8]
    h_cols, made_down, made_up, sem = refs[-4:]
    step, last = pl.program_id(0), pl.num_programs(0) - 1
    slot = step % 2
    width = h_ref.shape[1]

    def copies(c, at):
        if direct:
            owners, rows = made_down.shape[1], made_down.shape[2]
            part = made_up.shape[2]
            there = (
                goal_down.at[pl.ds(c * owners, owners), pl.ds(0, rows), :],
                goal_up.at[:, pl.ds(pl.multiple_of(rows + c * part, part), part), :],
            )
        else:
            span = pl.ds(pl.multiple_of(c * width, width), width)
            there = (goal_down.at[span, :], goal_up.at[:, span])
        return [
            pltpu.make_async_copy(made_down.at[at], there[0], sem.at[0, at]),
            pltpu.make_async_copy(made_up.at[at], there[1], sem.at[1, at]),
        ]

    @pl.when(step == 0)
    def _():
        h_cols[...] = h_ref[...].T

    up = up_ref[...].reshape(width, width)
    down = down_ref[...].reshape(width, width)
    for r in range(0, h_ref.shape[0], block):
        rows = pl.ds(r, block)
        pre = jnp.dot(h_ref[rows, :], up, preferred_element_type=F32)
        grad = lax.dot_general(dy_ref[rows, :], down, COLS_LAST, preferred_element_type=F32)
        below = 0.5 + 0.5 * lax.erf(pre * 0.5**0.5)
        bell = jnp.exp(pre * pre * -0.5) * (2.0 * math.pi) ** -0.5
        f_ref[rows, :] = (pre * below).astype(BF)
        da_ref[rows, :] = (grad * (below + pre * bell)).astype(BF)

    @pl.when(step >= 2)
    def _():
        for copy in copies(step - 2, slot):
            copy.wait()

    grad = lax.dot_general(f_ref[...], dy_ref[...], ROWS_FIRST, preferred_element_type=F32)
    made_down[slot] = grad.astype(BF).reshape(made_down.shape[1:])
    grad = jnp.dot(h_cols[...], da_ref[...], preferred_element_type=F32)
    made_up[slot] = grad.astype(BF).reshape(made_up.shape[1:])
    for copy in copies(step, slot):
        copy.start()

    @pl.when(step == last)
    def _():
        for copy in copies(step - 1, 1 - slot) + copies(step, slot):
            copy.wait()


def feed_weights(packed):
    owners, eight, width = packed.shape
    part = eight // 8
    if part % 16 == 0:
        return (packed, packed), (
            pl.BlockSpec((owners, part, width), lambda c: (0, 4 + c, 0)),
            pl.BlockSpec((owners // 4, 4 * part, width), lambda c: (c, 0, 0)),
        )
    down = packed[:, : 4 * part].reshape(4 * width, width)
    up = packed[:, 4 * part :].reshape(owners, 4, part, width)
    up = up.transpose(0, 2, 1, 3).reshape(width, 4 * width)
    return (up, down), (
        pl.BlockSpec((width, width), lambda c: (0, c)),
        pl.BlockSpec((width, width), lambda c: (c, 0)),
    )


def feed_forward(h, dy, weights, specs, owners):
    count, width = h.shape
    part = width // owners
    hidden = 4 * width
    direct = part % 16 == 0
    whole = pl.BlockSpec((count, width), lambda c: (0, 0))
    column = pl.BlockSpec((count, width), lambda c: (0, c))
    anywhere = pl.BlockSpec(memory_space=pl.ANY)
    if direct:
        made = [(owners // 4, 4 * part, width), (owners, part, width)]
        goals = [jax.ShapeDtypeStruct((owners, 8 * part, width), BF)]
    else:
        made = [(width, width)] * 2
        goals = [
            jax.ShapeDtypeStruct((hidden, width), BF),
            jax.ShapeDtypeStruct((width, hidden), BF),
        ]
    f, da, *grads = pl.pallas_call(
        functools.partial(feed_body, block=count // 3, direct=direct),
        grid=(4,),
        in_specs=[whole, whole, *specs],
        out_specs=[column, column] + [anywhere] * len(goals),
        out_shape=[jax.ShapeDtypeStruct((count, hidden), BF)] * 2 + goals,
        scratch_shapes=[pltpu.VMEM((width, count), BF)]
        + [pltpu.VMEM((2, *shape), BF) for shape in made]
        + [pltpu.SemaphoreType.DMA((2, 2))],
        compiler_params=pltpu.CompilerParams(
            dimension_semantics=("arbitrary",), vmem_limit_bytes=VMEM_BYTES
        ),
        cost_estimate=pl.CostEstimate(
            flops=8 * count * width * hidden,
            transcendentals=2 * count * hidden,
            bytes_accessed=4 * (count + 2 * width) * (hidden + width),
        ),
    )(h, dy, *weights)
    if direct:
        return f, da, grads[0]
    down, up = grads
    up = up.reshape(owners, part, 4, width).transpose(0, 2, 1, 3)
    packed = jnp.concatenate(
        [down.reshape(owners, 4 * part, width), up.reshape(owners, 4 * part, width)], 1
    )
    return f, da, packed


def turn(x, tables, sign=1.0):
    cosine, ahead, behind = tables
    half = ROT // 2
    return (
        x * cosine
        + pltpu.roll(x, 2 * HD - half, 1) * (sign * ahead)
        + pltpu.roll(x, half, 1) * (sign * behind)
    )


def key_only(tables):
    cosine, ahead, behind = tables
    first = lax.broadcasted_iota(jnp.int32, cosine.shape, 1) < HD
    return jnp.where(first, cosine, 1.0), jnp.where(first, ahead, 0.0), jnp.where(first, behind, 0.0)


def turn_tables(first, count):
    cosine, sine = angles(first, count)
    half = ROT // 2
    rest = jnp.zeros((count, HD - ROT), F32)
    none = jnp.zeros((count, half), F32)
    cosine = jnp.concatenate([cosine, rest + 1.0], 1)
    ahead = jnp.concatenate([-sine[:, :half], none, rest], 1)
    behind = jnp.concatenate([none, sine[:, half:], rest], 1)
    return [jnp.concatenate([t, t], 1) for t in (cosine, ahead, behind)]


def normed_rows(x):
    mean = jnp.mean(x, -1, keepdims=True)
    centered = x - mean
    scale = lax.rsqrt(jnp.mean(centered * centered, -1, keepdims=True) + EPS_NORM)
    return centered * scale, scale


def norm_rows_of(small_ref):
    return small_ref[:, pl.ds(2 * HD, 2 * HD)].astype(F32).T


def entry_body(x_ref, small_ref, cos_ref, ahead_ref, behind_ref, h1_ref, h2_ref, kv_ref, *, block):
    params = norm_rows_of(small_ref)
    weight = small_ref[:, pl.ds(0, 2 * HD)]
    for r in range(0, x_ref.shape[1], block):
        rows = pl.ds(r, block)
        normed, _ = normed_rows(x_ref[0, rows, :].astype(F32))
        first = (normed * params[0:1] + params[1:2]).astype(BF)
        h1_ref[0, rows, :] = first
        h2_ref[0, rows, :] = (normed * params[2:3] + params[3:4]).astype(BF)
        pair = jnp.dot(first, weight, preferred_element_type=F32)
        tables = key_only([t[rows, :] for t in (cos_ref, ahead_ref, behind_ref)])
        kv_ref[0, rows, :] = turn(pair, tables).astype(BF)


def entry(x, small, tables):
    batch, local, width = x.shape
    rows = pl.BlockSpec((1, local, width), lambda b: (b, 0, 0))
    table = pl.BlockSpec((local, 2 * HD), lambda b: (0, 0))
    return pl.pallas_call(
        functools.partial(entry_body, block=local // 3),
        grid=(batch,),
        in_specs=[rows, pl.BlockSpec(small.shape, lambda b: (0, 0)), table, table, table],
        out_specs=[rows, rows, pl.BlockSpec((1, local, 2 * HD), lambda b: (b, 0, 0))],
        out_shape=[jax.ShapeDtypeStruct(x.shape, BF)] * 2
        + [jax.ShapeDtypeStruct((batch, local, 2 * HD), BF)],
        compiler_params=pltpu.CompilerParams(
            dimension_semantics=("arbitrary",), vmem_limit_bytes=VMEM_BYTES
        ),
        cost_estimate=pl.CostEstimate(
            flops=4 * batch * local * width * HD,
            transcendentals=batch * local,
            bytes_accessed=8 * batch * local * width,
        ),
    )(x, small, *tables)


def query_body(h_ref, dy_ref, weight_ref, cos_ref, ahead_ref, behind_ref, q_ref, do_ref):
    mixed = jnp.dot(h_ref[0], weight_ref[:, pl.ds(0, D)], preferred_element_type=F32)
    tables = cos_ref[...], ahead_ref[...], behind_ref[...]
    for c in range(0, D, 2 * HD):
        q = turn(mixed[:, c : c + 2 * HD], tables).astype(BF)
        q_ref[0, :, pl.ds(c, 2 * HD)] = q * BF(HD ** (-0.5))
    do_ref[0] = lax.dot_general(
        dy_ref[0], weight_ref[:, pl.ds(D, D)], COLS_LAST, preferred_element_type=F32
    ).astype(BF)


def queries(h, dy, middle, tables):
    batch, local, width = h.shape
    rows = pl.BlockSpec((1, local, width), lambda b: (b, 0, 0))
    table = pl.BlockSpec((local, 2 * HD), lambda b: (0, 0))
    return pl.pallas_call(
        query_body,
        grid=(batch,),
        in_specs=[rows, rows, pl.BlockSpec(middle.shape, lambda b: (0, 0)), table, table, table],
        out_specs=[rows, rows],
        out_shape=[jax.ShapeDtypeStruct(h.shape, BF)] * 2,
        compiler_params=pltpu.CompilerParams(
            dimension_semantics=("arbitrary",), vmem_limit_bytes=VMEM_BYTES
        ),
        cost_estimate=pl.CostEstimate(
            flops=4 * batch * local * width * width,
            transcendentals=0,
            bytes_accessed=8 * batch * local * width,
        ),
    )(h, dy, middle, *tables)


def back_body(
    core_of, weight_of, x_ref, cot_ref, h_ref, o_ref, dq_ref, dh2_ref, middle_ref, small_ref,
    cos_ref, ahead_ref, behind_ref, *refs, devices,
):
    pair_refs, refs = refs[: devices * weight_of.shape[0]], refs[devices * weight_of.shape[0] :]
    dx_ref, *grad_refs, acc, norm_acc, pair_acc = refs
    b, last = pl.program_id(0), pl.num_programs(0) - 1
    tables = cos_ref[...], ahead_ref[...], behind_ref[...]
    params = norm_rows_of(small_ref)
    dy = cot_ref[0].astype(F32) * weight_of[b]
    dy_low = dy.astype(BF)
    for at in range(weight_of.shape[0]):

        @pl.when(b == at)
        def _(parts=pair_refs[devices * at : devices * (at + 1)]):
            total = parts[0][...].astype(F32)
            for part in parts[1:]:
                total = total + part[...].astype(F32)
            pair_acc[...] = total.astype(BF).astype(F32)

    pair = turn(pair_acc[...], key_only(tables), -1.0).astype(BF)
    turned = [
        turn(dq_ref[0, :, pl.ds(c, 2 * HD)].astype(F32), tables, -1.0).astype(BF)
        for c in range(0, D, 2 * HD)
    ]
    dz = jnp.concatenate(turned + [pair], 1)
    wide = dz.shape[1]
    made = lax.dot_general(h_ref[0], dz, ROWS_FIRST, preferred_element_type=F32)
    made_out = lax.dot_general(o_ref[0], dy_low, ROWS_FIRST, preferred_element_type=F32)

    @pl.when(b == 0)
    def _():
        acc[:, pl.ds(0, wide)] = made
        acc[:, pl.ds(wide, D)] = made_out
        norm_acc[...] = jnp.zeros_like(norm_acc)

    @pl.when(b > 0)
    def _():
        acc[:, pl.ds(0, wide)] += made
        acc[:, pl.ds(wide, D)] += made_out

    weights = jnp.concatenate([middle_ref[:, pl.ds(0, D)], small_ref[:, pl.ds(0, 2 * HD)]], 1)
    dh1 = lax.dot_general(dz, weights, COLS_LAST, preferred_element_type=F32)
    dh2 = dh2_ref[0]
    normed, scale = normed_rows(x_ref[0].astype(F32))
    norm_acc[0:1] += jnp.sum(dh1 * normed, 0, keepdims=True)
    norm_acc[1:2] += jnp.sum(dh1, 0, keepdims=True)
    norm_acc[2:3] += jnp.sum(dh2 * normed, 0, keepdims=True)
    norm_acc[3:4] += jnp.sum(dh2, 0, keepdims=True)
    inner = dh1 * params[0:1] + dh2 * params[2:3]
    inner = inner - jnp.mean(inner, -1, keepdims=True) - normed * jnp.mean(
        inner * normed, -1, keepdims=True
    )
    dx_ref[0] = (dy + scale * inner).astype(BF)

    @pl.when(b == last)
    def _():
        acc[:, pl.ds(wide + D, 2 * HD)] = norm_acc[...].T
        if len(grad_refs) == 1:
            grad_refs[0][...] = acc[...].astype(BF)
            return
        send_ref, keep_ref = grad_refs
        pairs, part, _ = send_ref.shape
        for p in range(pairs):
            for ref, core in ((send_ref, 1 - core_of[0]), (keep_ref, core_of[0])):
                rows = pl.ds(pl.multiple_of((2 * p + core) * part, part), part)
                ref[p] = acc[rows, :].astype(ref.dtype)


def back(core, row_weight, owners, x, cot, h, o, dq, pairs, dh2, middle, small, tables):
    batch, local, width = x.shape
    rows = pl.BlockSpec((1, local, width), lambda b, *s: (b, 0, 0))
    table = pl.BlockSpec((local, 2 * HD), lambda b, *s: (0, 0))
    columns = 2 * width + 4 * HD
    part = width // owners
    if part % 16 == 0:
        half = (owners // 2, part, columns)
        made = [jax.ShapeDtypeStruct(half, BF), jax.ShapeDtypeStruct(half, F32)]
    else:
        made = [jax.ShapeDtypeStruct((width, columns), BF)]
    return pl.pallas_call(
        functools.partial(back_body, devices=len(pairs[0])),
        grid_spec=pltpu.PrefetchScalarGridSpec(
            num_scalar_prefetch=2,
            grid=(batch,),
            in_specs=[rows] * 6
            + [pl.BlockSpec(w.shape, lambda b, *s: (0, 0)) for w in (middle, small)]
            + [table] * (3 + sum(len(parts) for parts in pairs)),
            out_specs=[rows]
            + [pl.BlockSpec(m.shape, lambda b, *s, n=len(m.shape): (0,) * n) for m in made],
            scratch_shapes=[
                pltpu.VMEM((width, columns), F32),
                pltpu.VMEM((2 * HD, width), F32),
                pltpu.VMEM((local, 2 * HD), F32),
            ],
        ),
        out_shape=[jax.ShapeDtypeStruct(x.shape, BF), *made],
        compiler_params=pltpu.CompilerParams(
            dimension_semantics=("arbitrary",), vmem_limit_bytes=VMEM_BYTES
        ),
        cost_estimate=pl.CostEstimate(
            flops=6 * batch * local * width * width,
            transcendentals=batch * local,
            bytes_accessed=16 * batch * local * width,
        ),
    )(
        core, row_weight, x, cot, h, o, dq, dh2, middle, small, *tables,
        *[part for parts in pairs for part in parts],
    )


def sum_body(a_ref, w_ref, out_ref):
    width = out_ref.shape[1]
    part = lax.dot_general(
        a_ref[...], w_ref[...].reshape(width, width), COLS_LAST, preferred_element_type=F32
    )

    @pl.when(pl.program_id(0) == 0)
    def _():
        out_ref[...] = part

    @pl.when(pl.program_id(0) > 0)
    def _():
        out_ref[...] += part


def up_back(da, weights, specs):
    count, hidden = da.shape
    width = hidden // 4
    return pl.pallas_call(
        sum_body,
        grid=(4,),
        in_specs=[pl.BlockSpec((count, width), lambda c: (0, c)), specs[0]],
        out_specs=pl.BlockSpec((count, width), lambda c: (0, 0)),
        out_shape=jax.ShapeDtypeStruct((count, width), F32),
        compiler_params=pltpu.CompilerParams(
            dimension_semantics=("arbitrary",), vmem_limit_bytes=VMEM_BYTES
        ),
        cost_estimate=pl.CostEstimate(
            flops=2 * count * width * hidden,
            transcendentals=0,
            bytes_accessed=2 * count * hidden + 4 * count * width + 2 * width * hidden,
        ),
    )(da, weights[0])


def output_body(x_ref, o_ref, out_w_ref, f_ref, w_ref, y_ref, acc):
    step, last = pl.program_id(0), pl.num_programs(0) - 1
    width = acc.shape[1]
    part = jnp.dot(f_ref[...], w_ref[...].reshape(width, width), preferred_element_type=F32)

    @pl.when(step == 0)
    def _():
        heads = jnp.dot(o_ref[...], out_w_ref[...], preferred_element_type=F32)
        acc[...] = x_ref[...].astype(F32) + heads + part

    @pl.when(step > 0)
    def _():
        acc[...] += part

    @pl.when(step == last)
    def _():
        y_ref[...] = acc[...].astype(BF)


def output(x, o, middle, f, weights, specs):
    count, hidden = f.shape
    width = hidden // 4
    whole = pl.BlockSpec((count, width), lambda c: (0, 0))
    return pl.pallas_call(
        output_body,
        grid=(4,),
        in_specs=[
            whole,
            whole,
            pl.BlockSpec((width, width), lambda c: (0, 1)),
            pl.BlockSpec((count, width), lambda c: (0, c)),
            specs[1],
        ],
        out_specs=whole,
        out_shape=jax.ShapeDtypeStruct((count, width), BF),
        scratch_shapes=[pltpu.VMEM((count, width), F32)],
        compiler_params=pltpu.CompilerParams(
            dimension_semantics=("arbitrary",), vmem_limit_bytes=VMEM_BYTES
        ),
        cost_estimate=pl.CostEstimate(
            flops=2 * count * width * (hidden + width),
            transcendentals=0,
            bytes_accessed=2 * (count + width) * hidden + 6 * count * width,
        ),
    )(x, o, middle, f, weights[1])


def adam_store(weight_ref, first_ref, second_ref, grad, outs, rate, decay):
    results = adam_update(weight_ref[...], first_ref[...], second_ref[...], grad, rate, decay)
    for out_ref, result in zip(outs, results):
        out_ref[...] = result


def adam_body(seq_at, factor_ref, up_grad_ref, down_grad_ref, *refs):
    parts, refs, joined = refs[:4], refs[4:-1], refs[-1]
    factor = factor_ref[0, 0]
    qkv, out, up, down, norm = [refs[3 * i : 3 * i + 3] for i in range(5)]
    outs = refs[15:]
    qkv_out, out_out, up_out, down_out, norm_out = [outs[3 * i : 3 * i + 3] for i in range(5)]
    adam_store(*up, up_grad_ref[...].astype(F32) * factor, up_out, RATE_SMALL, DECAY)
    adam_store(*down, down_grad_ref[...].astype(F32) * factor, down_out, RATE_SMALL, DECAY)

    step = pl.program_id(0)

    @pl.when(step == 0)
    def _():
        for mask, ref in enumerate(parts):
            joined[seq_at[0] ^ mask] = unpack_quarter(ref)

    rest = joined[step]
    wide = qkv[0].shape[1]
    adam_store(*qkv, rest[:, :wide] * factor, qkv_out, RATE_SMALL, DECAY)
    adam_store(*out, rest[:, wide : wide + D] * factor, out_out, RATE_LARGE, DECAY)

    @pl.when(step == pl.num_programs(0) - 1)
    def _():
        norms = joined[:, :, pl.ds(wide + D, 2 * HD)].reshape(-1, 2 * HD)
        adam_store(*norm, norms.T[:4] * factor, norm_out, RATE_NORM, 0.0)


def adam_all(seq_at, factor, feed, rest, qkv, out, up, down, norm):
    part, hidden = up[0].shape
    width = hidden // 4
    column = pl.BlockSpec((part, width), lambda c, p: (0, c))
    row = pl.BlockSpec((part, width), lambda c, p: (c, 0))

    def quarter(x):
        return pl.BlockSpec((part // 4, x.shape[1]), lambda c, p: (c, 0))

    def whole(x):
        return pl.BlockSpec(x.shape, lambda c, p: (0, 0))

    states = [*qkv, *out, *up, *down, *norm]
    specs = (
        [quarter(x) for x in qkv + out] + [column] * 3 + [row] * 3 + [whole(x) for x in norm]
    )
    return pl.pallas_call(
        adam_body,
        grid_spec=pltpu.PrefetchScalarGridSpec(
            num_scalar_prefetch=1,
            grid=(4,),
            in_specs=[
                pl.BlockSpec(memory_space=pltpu.SMEM),
                pl.BlockSpec((part, width), lambda c, p: (4 + c, 0)),
                row,
                *[whole(x) for x in rest],
                *specs,
            ],
            out_specs=specs,
            scratch_shapes=[pltpu.VMEM((4, rest[0].shape[0], rest[0].shape[1] - 2 * HD), F32)],
        ),
        out_shape=[jax.ShapeDtypeStruct(x.shape, F32) for x in states],
        compiler_params=pltpu.CompilerParams(
            dimension_semantics=("arbitrary",), vmem_limit_bytes=VMEM_BYTES
        ),
    )(seq_at, factor, feed, feed, *rest, *states)


def swap(x, axis, mask):
    return lax.ppermute(x, axis, [(i, i ^ mask) for i in range(lax.axis_size(axis))])


def local_call(body, at, inputs, shapes, scratch=()):
    return pl.pallas_call(
        body,
        grid_spec=pltpu.PrefetchScalarGridSpec(
            num_scalar_prefetch=1,
            grid=(1,),
            in_specs=[pl.BlockSpec(a.shape, lambda i, p, n=a.ndim: (0,) * n) for a in inputs],
            out_specs=[pl.BlockSpec(s, lambda i, p, n=len(s): (0,) * n) for s, _ in shapes],
            scratch_shapes=list(scratch),
        ),
        out_shape=[jax.ShapeDtypeStruct(s, kind) for s, kind in shapes],
        compiler_params=pltpu.CompilerParams(
            dimension_semantics=("arbitrary",), vmem_limit_bytes=VMEM_BYTES // 3
        ),
    )(at, *inputs)


def split_chips(at, keep, came, send_left, send_right, keep_left, keep_right):
    x, y = at[0], at[1]
    half = send_left.shape[2]
    left, right = pl.ds(0, half), pl.ds(half, half)
    for i in range(2):
        for ref, block, columns in (
            (send_left, 2 * i + 1 - x, left),
            (keep_left, 2 * i + x, left),
            (send_right, 2 * (1 - y) + i, right),
            (keep_right, 2 * y + i, right),
        ):
            total = keep[block, :, columns] + came[block, :, columns].astype(F32)
            ref[i] = total.astype(ref.dtype)


def split_last(at, left, right, a, b, send_left, send_right, keep_left, keep_right):
    x, y = at[0], at[1]
    for ref, keep, came, block in (
        (send_left, left, a, 1 - y),
        (keep_left, left, a, y),
        (send_right, right, b, 1 - x),
        (keep_right, right, b, x),
    ):
        ref[...] = (keep[block] + came[block].astype(F32)).astype(ref.dtype)


def split_seq(at, left, right, a, b, one, two, three, keep, total):
    half = left.shape[1]
    quarters, rows, _ = total.shape
    total[:, :, pl.ds(0, half)] = (left[...] + a[...].astype(F32)).reshape(quarters, rows, half)
    total[:, :, pl.ds(half, half)] = (right[...] + b[...].astype(F32)).reshape(quarters, rows, half)
    seq = at[2]
    keep[...] = total[seq]
    for mask, ref in ((1, one), (2, two), (3, three)):
        ref[...] = total[seq ^ mask].astype(BF)


def pack_quarter(at, keep, one, two, three, packed):
    total = keep[...]
    for ref in (one, two, three):
        total = total + ref[...].astype(F32)
    wide = total.shape[1]
    packed[:, pl.ds(0, wide)] = total.astype(BF)
    pair = total[:, D : D + 2 * HD]
    packed[:, pl.ds(wide, 2 * HD)] = (pair - pair.astype(BF).astype(F32)).astype(BF)


def unpack_quarter(ref):
    wide = ref.shape[1] - 2 * HD
    pair = pl.ds(D, 2 * HD)
    after = D + 2 * HD
    return jnp.concatenate(
        [
            ref[:, pl.ds(0, D)].astype(F32),
            ref[:, pair].astype(F32) + ref[:, pl.ds(wide, 2 * HD)].astype(F32),
            ref[:, pl.ds(after, wide - after)].astype(F32),
        ],
        1,
    )


def add_squares(at, *refs):
    *quarters, feed, squares = refs
    total = jnp.zeros(squares.shape, F32)
    for grad in [unpack_quarter(ref) for ref in quarters] + [feed[...].astype(F32)]:
        parts = jnp.sum(jnp.square(grad), 0, keepdims=True)
        for c in range(0, grad.shape[1], 2 * HD):
            total = total + parts[:, c : c + 2 * HD]
    squares[...] = total


def beside(sends, work=lambda: (), inputs=()):
    flat, inputs = lax.optimization_barrier(([x for x, _, _ in sends], inputs))
    came = [swap(x, axis, mask) for x, (_, axis, mask) in zip(flat, sends)]
    return lax.optimization_barrier((came, work(*inputs)))


def batch_sum(at, send, keep, work, inputs):
    (came,), _ = beside([(send, "batch", 1)])
    _, r, c = keep.shape
    two, one, quarter = (2, r, c // 2), (r, c // 2), (r // 4, c)
    send_left, send_right, left, right = local_call(
        split_chips, at, [keep, came], [(two, BF), (two, BF), (two, F32), (two, F32)]
    )
    (a, b), _ = beside([(send_left, "batch", 2), (send_right, "batch", 4)])
    send_left, send_right, left, right = local_call(
        split_last, at, [left, right, a, b], [(one, BF), (one, BF), (one, F32), (one, F32)]
    )
    (a, b), _ = beside([(send_left, "batch", 4), (send_right, "batch", 2)])
    *sends, keep = local_call(
        split_seq,
        at,
        [left, right, a, b],
        [(quarter, BF)] * 3 + [(quarter, F32)],
        [pltpu.VMEM((4, *quarter), F32)],
    )
    came, result = beside([(x, "seq", m + 1) for m, x in enumerate(sends)], work, inputs)
    (own,) = local_call(pack_quarter, at, [keep, *came], [((r // 4, c + 2 * HD), BF)])
    came, _ = beside([(own, "seq", mask) for mask in (1, 2, 3)])
    return [own, *came], result


def shift(x, by):
    count = lax.axis_size("seq")
    return lax.ppermute(x, "seq", [(s, s + by) for s in range(count) if 0 <= s + by < count])


def shards(
    tokens,
    cotangent,
    tags,
    loss_weights,
    w_qkv,
    m_qkv,
    v_qkv,
    w_out,
    m_out,
    v_out,
    w_up,
    m_up,
    v_up,
    w_down,
    m_down,
    v_down,
    norm_params,
    m_norm,
    v_norm,
):
    owners = lax.axis_size("batch")
    seq_count = lax.axis_size("seq")
    seq_at = lax.axis_index("seq")
    seq_rows, local, width = tokens.shape
    count = seq_rows * local
    part = w_qkv.shape[0]
    fence = lax.optimization_barrier

    small = jnp.concatenate(
        [w_qkv[:, D:], norm_params.T, jnp.zeros((part, 2 * HD - 4), F32)], 1
    ).astype(BF)
    small = lax.all_gather(small, "batch", axis=0, tiled=True)
    middle = jnp.concatenate([w_qkv[:, :D], w_out], 1).astype(BF)
    middle = lax.all_gather(middle, "batch", axis=0, tiled=True)
    packed = jnp.concatenate([w_down] + [w_up[:, D * i : D * (i + 1)] for i in range(4)], 0)
    packed, small = fence((packed.astype(BF), small))
    packed = lax.all_gather(packed, "batch", axis=0, tiled=True).reshape(owners, 8 * part, D)
    weights, specs = feed_weights(packed)

    tables = turn_tables(seq_at * local, local)
    subsets = jnp.arange(loss_weights.shape[0])
    row_weight = jnp.sum(
        jnp.where(tags[:, None] == subsets[None, :], loss_weights[None, :], 0.0), -1
    )
    grad_low = (cotangent.astype(F32) * row_weight[:, None, None]).astype(BF)

    first_low, second_low, pair = entry(tokens, small, tables)
    query, grad_heads = queries(first_low, grad_low, middle, tables)

    def gather_pair(own):
        return [own] + [shift(own, by) for by in range(1, seq_count)]

    arrived, query = fence((gather_pair(pair[0]), query))
    place = jnp.reshape(seq_at, (1,)).astype(jnp.int32)

    state, came = (), []
    for at in range(seq_rows):
        if at == seq_rows // 2:
            second_low, state = fence((second_low, state))
            active_low, grad_up_pre, grad_feed = feed_forward(
                second_low.reshape(count, D), grad_low.reshape(count, D), weights, specs, owners
            )
            feed_sum = lax.psum_scatter(
                grad_feed.reshape(owners * 8 * part, D), "batch", scatter_dimension=0, tiled=True
            )
            state, grad_up_pre = fence((state, grad_up_pre))
        keys = arrived
        if at + 1 < seq_rows:
            own, keys = fence((pair[at + 1], keys))
            arrived = gather_pair(own)
        heads, grad_query, *grad_pair = attention(place, query, grad_heads, keys, at, state)
        state = heads, grad_query
        came.append([shift(g, -by) if by else g for by, g in enumerate(grad_pair)])
        if at + 1 < seq_rows:
            arrived, state = fence((arrived, state))
    heads, grad_query = state

    grad_up_pre, heads = fence((grad_up_pre, heads))
    grad_second = up_back(grad_up_pre, weights, specs)
    quarter = (-(-part // 4), w_qkv.shape[1] + D + 4 * HD)
    blanks = [jnp.zeros(quarter, BF)] * 4
    came, grad_second, feed_sum, blanks = fence((came, grad_second, feed_sum, blanks))
    feed_sum = lax.psum(feed_sum, "seq")

    def input_side():
        return back(
            jnp.reshape(lax.axis_index("batch") % 2, (1,)),
            row_weight,
            owners,
            tokens,
            cotangent,
            first_low,
            heads,
            grad_query,
            came,
            grad_second.reshape(seq_rows, local, D),
            middle,
            small,
            tables,
        )

    def output_side(x, o, w, f):
        return output(x, o, w, f, weights, specs)

    output_inputs = tokens.reshape(count, D), heads.reshape(count, D), middle, active_low

    if owners == 8 and seq_count == 4:
        batch_at = lax.axis_index("batch")
        at = jnp.stack([(batch_at // 2) % 2, batch_at // 4, seq_at])

        def rest_of_layer(_, carry):
            input_grad, send, keep = input_side()
            parts, layer_out = batch_sum(at, send, keep, output_side, output_inputs)
            return input_grad, layer_out, parts

        unused = (
            second_low,
            query.reshape(count, D),
            blanks,
        )
        once = 1 + jnp.minimum(tags[0], 0)
        input_grad, layer_out, rest = lax.fori_loop(0, once, rest_of_layer, unused)
        feed_sum, rest = fence((feed_sum, rest))
        (squares,) = local_call(add_squares, at, [*rest, feed_sum], [((1, 2 * HD), F32)])
        total_squares = jnp.sum(lax.all_gather(squares, "batch"))
    else:
        input_grad, rest = input_side()
        layer_out = output_side(*output_inputs)
        rest = lax.psum_scatter(rest.astype(F32), "batch", scatter_dimension=0, tiled=True)
        rest = lax.psum(rest, "seq")
        squares = [jnp.sum(jnp.square(x.astype(F32))) for x in (rest, feed_sum)]
        total_squares = lax.psum(sum(squares), "batch")
    layer_out = layer_out.reshape(seq_rows, local, D)
    grad_norm = jnp.sqrt(total_squares)
    factor = CLIP_NORM / jnp.maximum(grad_norm, CLIP_NORM)
    states = (
        (w_qkv, m_qkv, v_qkv),
        (w_out, m_out, v_out),
        (w_up, m_up, v_up),
        (w_down, m_down, v_down),
        (norm_params, m_norm, v_norm),
    )
    if isinstance(rest, list):
        results = adam_all(at[2:], factor.reshape(1, 1), feed_sum, rest, *states)
    else:
        qkv_width = w_qkv.shape[1]
        down_sum, up_sum = feed_sum[: 4 * part], feed_sum[4 * part :]
        up_sum = up_sum.astype(F32).reshape(4, part, D).transpose(1, 0, 2)
        grads = (
            rest[:, :qkv_width],
            rest[:, qkv_width : qkv_width + D],
            up_sum.reshape(part, 4 * D),
            down_sum.astype(F32),
            rest[:, qkv_width + D : qkv_width + D + 4].T,
        )
        rates = (RATE_SMALL, RATE_LARGE, RATE_SMALL, RATE_SMALL, RATE_NORM)
        decays = (DECAY, DECAY, DECAY, DECAY, 0.0)
        results = []
        for three, grad, rate, decay in zip(states, grads, rates, decays):
            results.extend(adam_update(*three, grad * factor, rate, decay))
    return (layer_out, input_grad, grad_norm, *results)


def solution(mesh):
    in_specs = (
        P("batch", "seq", None),
        P("batch", "seq", None),
        P("batch"),
        P(),
        P("batch", None),
        P("batch", None),
        P("batch", None),
        P("batch", None),
        P("batch", None),
        P("batch", None),
        P("batch", None),
        P("batch", None),
        P("batch", None),
        P("batch", None),
        P("batch", None),
        P("batch", None),
        P(None, "batch"),
        P(None, "batch"),
        P(None, "batch"),
    )
    out_specs = (
        P("batch", "seq", None),
        P("batch", "seq", None),
        P(),
        P("batch", None),
        P("batch", None),
        P("batch", None),
        P("batch", None),
        P("batch", None),
        P("batch", None),
        P("batch", None),
        P("batch", None),
        P("batch", None),
        P("batch", None),
        P("batch", None),
        P("batch", None),
        P(None, "batch"),
        P(None, "batch"),
        P(None, "batch"),
    )
    return jax.shard_map(shards, mesh=mesh, in_specs=in_specs, out_specs=out_specs, check_vma=False)
```

```python
import functools
import math

import jax
import jax.numpy as jnp
from jax import lax
from jax.experimental import pallas as pl
from jax.experimental.pallas import tpu as pltpu
from jax.sharding import PartitionSpec as P

D = 768
H = 12
HD = 64
ROT = 16
STEP = 10


EPS_NORM = 1e-05
BETA_ONE = 0.9
BETA_TWO = 0.999
ADAM_EPS = 1e-08
CLIP_NORM = 1.0
RATE_SMALL = 0.02
RATE_LARGE = 0.2
RATE_NORM = 1.0
DECAY = 0.1
ROWS_FIRST = (((0,), (0,)), ((), ()))
COLS_LAST = (((1,), (1,)), ((), ()))


def angles(first, count):
    place = (first + jnp.arange(count)).astype(jnp.float32)
    inverse = 10000.0 ** (-jnp.arange(0, ROT, 2).astype(jnp.float32) / ROT)
    turn = place[:, None] * inverse[None, :]
    turn = jnp.concatenate([turn, turn], -1)
    return (jnp.cos(turn), jnp.sin(turn))


def adam_update(weight, first, second, grad, rate, decay):
    first_new = BETA_ONE * first + (1.0 - BETA_ONE) * grad
    second_new = BETA_TWO * second + (1.0 - BETA_TWO) * grad * grad
    step_one = first_new / (1.0 - BETA_ONE**STEP)
    step_two = second_new / (1.0 - BETA_TWO**STEP)
    weight_new = weight - rate * (step_one / (jnp.sqrt(step_two) + ADAM_EPS) + decay * weight)
    return (weight_new, first_new, second_new)


BF = jnp.bfloat16
F32 = jnp.float32
ROWS = 128
KEYS = 384
VMEM_BYTES = 60 << 20


def attention_body(
    place,
    q_ref,
    do_ref,
    *refs,
    local,
    devices,
):
    kv_refs, refs = refs[:devices], refs[-10 - devices :]
    o_ref, dq_ref, dkv_refs = refs[0], refs[1], refs[2 : 2 + devices]
    k_rows, v_rows, k_cols, v_cols, scores, out_acc, dq_acc, dkv_acc = refs[-8:]
    step = pl.program_id(0)
    chunks = scores.shape[0]
    wide = H * ROWS

    @pl.when(step == 0)
    def _():
        dkv_acc[...] = jnp.zeros_like(dkv_acc)
        for by, kv_ref in enumerate(kv_refs):

            @pl.when(place[0] >= by)
            def _(by=by, kv_ref=kv_ref):
                rows = pl.ds(pl.multiple_of((place[0] - by) * local, 8), local)
                dkv_acc[rows, :] = kv_ref[...].astype(F32)

        def prepare(j, carry):
            rows = pl.ds(pl.multiple_of(j * KEYS, KEYS), KEYS)
            pair = dkv_acc[rows, :].astype(BF)
            k_rows[rows, :] = pair[:, :HD]
            v_rows[rows, :] = pair[:, HD:]
            turned = pair.T
            k_cols[j] = turned[:HD]
            v_cols[j] = turned[HD:]
            dkv_acc[rows, :] = jnp.zeros((KEYS, 2 * HD), F32)
            return carry

        lax.fori_loop(0, chunks, prepare, 0)

    start = place[0] * local + step * ROWS
    last = jnp.minimum(start + ROWS - 1, (place[0] + 1) * local - 1)
    open_chunks = (start + 1) // KEYS
    all_chunks = last // KEYS + 1

    def heads_in_columns(x):
        turned = [x[:, 2 * HD * p : 2 * HD * (p + 1)].T for p in range(H // 2)]
        return jnp.concatenate([t[a : a + HD] for t in turned for a in (0, HD)], 1)

    def heads_in_rows(x):
        return jnp.concatenate([x[:, HD * h : HD * (h + 1)] for h in range(H)], 0)

    def heads_side_by_side(t):
        return jnp.concatenate(
            [
                jnp.concatenate(
                    [
                        t[:, 2 * p * ROWS : (2 * p + 1) * ROWS],
                        t[:, (2 * p + 1) * ROWS : (2 * p + 2) * ROWS],
                    ],
                    0,
                ).T
                for p in range(H // 2)
            ],
            1,
        )

    real = lax.broadcasted_iota(jnp.int32, (ROWS, D), 0) < local - step * ROWS
    q = jnp.where(real, q_ref[0], 0.0).astype(BF)
    do = jnp.where(real, do_ref[0], 0.0).astype(BF)
    q_cols = heads_in_columns(q)
    do_cols = heads_in_columns(do)
    blank = jnp.zeros((wide, HD), BF)
    q_side = jnp.concatenate([heads_in_rows(q), blank], 1)
    do_side = jnp.concatenate([blank, heads_in_rows(do)], 1)
    out_acc[...] = jnp.zeros_like(out_acc)
    dq_acc[...] = jnp.zeros_like(dq_acc)
    lane = lax.broadcasted_iota(jnp.int32, (1, wide), 1)
    query_at = start + (lane & (ROWS - 1))

    open_pairs, all_pairs, odd = open_chunks // 2, all_chunks // 2, all_chunks % 2

    def key_rows(j, count):
        return pl.ds(pl.multiple_of(j * KEYS, KEYS), count * KEYS)

    def columns(ref, j, count):
        return jnp.concatenate([ref[j + c] for c in range(count)], 1)

    def score_step(j, top, count, masked):
        raw = jnp.dot(k_rows[key_rows(j, count), :], q_cols, preferred_element_type=F32)
        if masked:
            key_at = j * KEYS + lax.broadcasted_iota(jnp.int32, (count * KEYS, wide), 0)
            raw = jnp.where(key_at <= query_at, raw, -1e30)
        scores[pl.ds(j, count)] = raw.reshape(count, KEYS, wide)
        return jnp.maximum(top, jnp.max(raw.reshape(count * KEYS // 8, 8, wide), 0))

    def value_step(j, total, count):
        expo = jnp.exp(scores[pl.ds(j, count)].reshape(count * KEYS, wide) - top)
        scores[pl.ds(j, count)] = expo.reshape(count, KEYS, wide)
        out_acc[...] += jnp.dot(
            columns(v_cols, j, count), expo.astype(BF), preferred_element_type=F32
        )
        return total + jnp.sum(expo.reshape(count * KEYS // 8, 8, wide), 0)

    def back_step(j, count):
        rows = key_rows(j, count)
        grad_probs = jnp.dot(v_rows[rows, :], do_cols, preferred_element_type=F32)
        probs = scores[pl.ds(j, count)].reshape(count * KEYS, wide) * share
        grad_scores = (probs * (grad_probs - inner)).astype(BF)
        dkv_acc[rows, :] += jnp.dot(
            grad_scores, q_side, preferred_element_type=F32
        ) + jnp.dot(probs.astype(BF), do_side, preferred_element_type=F32)
        dq_acc[...] += jnp.dot(
            columns(k_cols, j, count), grad_scores, preferred_element_type=F32
        )

    top = jnp.full((8, wide), -1e30, F32)
    top = lax.fori_loop(0, open_pairs, lambda p, t: score_step(2 * p, t, 2, False), top)
    top = lax.fori_loop(open_pairs, all_pairs, lambda p, t: score_step(2 * p, t, 2, True), top)
    top = lax.fori_loop(0, odd, lambda p, t: score_step(2 * all_pairs, t, 1, True), top)
    top = jnp.max(top, 0, keepdims=True)

    total = jnp.zeros((8, wide), F32)
    total = lax.fori_loop(0, all_pairs, lambda p, t: value_step(2 * p, t, 2), total)
    total = lax.fori_loop(0, odd, lambda p, t: value_step(2 * all_pairs, t, 1), total)
    share = 1.0 / jnp.sum(total, 0, keepdims=True)
    out = out_acc[...] * share
    inner = jnp.sum(out * do_cols.astype(F32), 0, keepdims=True)

    def back_pair(p, carry):
        back_step(2 * p, 2)
        return carry

    lax.fori_loop(0, all_pairs, back_pair, 0)

    @pl.when(odd != 0)
    def _():
        back_step(2 * all_pairs, 1)

    o_ref[0] = heads_side_by_side(out).astype(BF)
    dq_ref[0] = (heads_side_by_side(dq_acc[...]) * HD ** (-0.5)).astype(BF)

    @pl.when(step == pl.num_programs(0) - 1)
    def _():
        for by, dkv_ref in enumerate(dkv_refs):
            owner = jnp.maximum(place[0] - by, 0)
            rows = pl.ds(pl.multiple_of(owner * local, 8), local)
            dkv_ref[...] = dkv_acc[rows, :].astype(BF)


def attention(place, q, do, kv, at, earlier=()):
    local = q.shape[1]
    devices = len(kv)
    keys = devices * local
    chunks = -(-keys // KEYS)
    steps = -(-local // ROWS)
    wide = H * ROWS
    by_row = pl.BlockSpec((1, ROWS, D), lambda i, p: (at, i, 0))
    pairs = pl.BlockSpec((local, 2 * HD), lambda i, p: (0, 0))
    return pl.pallas_call(
        functools.partial(attention_body, local=local, devices=devices),
        grid_spec=pltpu.PrefetchScalarGridSpec(
            num_scalar_prefetch=1,
            grid=(steps,),
            in_specs=[by_row] * 2
            + [pairs] * devices
            + [pl.BlockSpec(memory_space=pl.ANY)] * len(earlier),
            out_specs=[by_row] * 2 + [pairs] * devices,
            scratch_shapes=[
                pltpu.VMEM((chunks * KEYS, HD), BF),
                pltpu.VMEM((chunks * KEYS, HD), BF),
                pltpu.VMEM((chunks, HD, KEYS), BF),
                pltpu.VMEM((chunks, HD, KEYS), BF),
                pltpu.VMEM((chunks, KEYS, wide), F32),
                pltpu.VMEM((HD, wide), F32),
                pltpu.VMEM((HD, wide), F32),
                pltpu.VMEM((chunks * KEYS, 2 * HD), F32),
            ],
        ),
        out_shape=[jax.ShapeDtypeStruct(q.shape, BF)] * 2
        + [jax.ShapeDtypeStruct((local, 2 * HD), BF)] * devices,
        input_output_aliases={3 + devices: 0, 4 + devices: 1} if earlier else {},
        compiler_params=pltpu.CompilerParams(
            dimension_semantics=("arbitrary",), vmem_limit_bytes=VMEM_BYTES
        ),
        cost_estimate=pl.CostEstimate(
            flops=12 * local * D * keys,
            transcendentals=local * H * keys,
            bytes_accessed=8 * local * D,
        ),
    )(place, q, do, *kv, *earlier)


def feed_body(*refs, block, direct):
    h_ref, dy_ref, up_ref, down_ref, f_ref, da_ref = refs[:6]
    goal_down, goal_up = (refs[6], refs[6]) if direct else refs[6:8]
    h_cols, made_down, made_up, sem = refs[-4:]
    step, last = pl.program_id(0), pl.num_programs(0) - 1
    slot = step % 2
    width = h_ref.shape[1]

    def copies(c, at):
        if direct:
            owners, rows = made_down.shape[1], made_down.shape[2]
            part = made_up.shape[2]
            there = (
                goal_down.at[pl.ds(c * owners, owners), pl.ds(0, rows), :],
                goal_up.at[:, pl.ds(pl.multiple_of(rows + c * part, part), part), :],
            )
        else:
            span = pl.ds(pl.multiple_of(c * width, width), width)
            there = (goal_down.at[span, :], goal_up.at[:, span])
        return [
            pltpu.make_async_copy(made_down.at[at], there[0], sem.at[0, at]),
            pltpu.make_async_copy(made_up.at[at], there[1], sem.at[1, at]),
        ]

    @pl.when(step == 0)
    def _():
        h_cols[...] = h_ref[...].T

    up = up_ref[...].reshape(width, width)
    down = down_ref[...].reshape(width, width)
    for r in range(0, h_ref.shape[0], block):
        rows = pl.ds(r, block)
        pre = jnp.dot(h_ref[rows, :], up, preferred_element_type=F32)
        grad = lax.dot_general(dy_ref[rows, :], down, COLS_LAST, preferred_element_type=F32)
        below = 0.5 + 0.5 * lax.erf(pre * 0.5**0.5)
        bell = jnp.exp(pre * pre * -0.5) * (2.0 * math.pi) ** -0.5
        f_ref[rows, :] = (pre * below).astype(BF)
        da_ref[rows, :] = (grad * (below + pre * bell)).astype(BF)

    @pl.when(step >= 2)
    def _():
        for copy in copies(step - 2, slot):
            copy.wait()

    grad = lax.dot_general(f_ref[...], dy_ref[...], ROWS_FIRST, preferred_element_type=F32)
    made_down[slot] = grad.astype(BF).reshape(made_down.shape[1:])
    grad = jnp.dot(h_cols[...], da_ref[...], preferred_element_type=F32)
    made_up[slot] = grad.astype(BF).reshape(made_up.shape[1:])
    for copy in copies(step, slot):
        copy.start()

    @pl.when(step == last)
    def _():
        for copy in copies(step - 1, 1 - slot) + copies(step, slot):
            copy.wait()


def feed_weights(packed):
    owners, eight, width = packed.shape
    part = eight // 8
    if part % 16 == 0:
        return (packed, packed), (
            pl.BlockSpec((owners, part, width), lambda c: (0, 4 + c, 0)),
            pl.BlockSpec((owners // 4, 4 * part, width), lambda c: (c, 0, 0)),
        )
    down = packed[:, : 4 * part].reshape(4 * width, width)
    up = packed[:, 4 * part :].reshape(owners, 4, part, width)
    up = up.transpose(0, 2, 1, 3).reshape(width, 4 * width)
    return (up, down), (
        pl.BlockSpec((width, width), lambda c: (0, c)),
        pl.BlockSpec((width, width), lambda c: (c, 0)),
    )


def feed_forward(h, dy, weights, specs, owners):
    count, width = h.shape
    part = width // owners
    hidden = 4 * width
    direct = part % 16 == 0
    whole = pl.BlockSpec((count, width), lambda c: (0, 0))
    column = pl.BlockSpec((count, width), lambda c: (0, c))
    anywhere = pl.BlockSpec(memory_space=pl.ANY)
    if direct:
        made = [(owners // 4, 4 * part, width), (owners, part, width)]
        goals = [jax.ShapeDtypeStruct((owners, 8 * part, width), BF)]
    else:
        made = [(width, width)] * 2
        goals = [
            jax.ShapeDtypeStruct((hidden, width), BF),
            jax.ShapeDtypeStruct((width, hidden), BF),
        ]
    f, da, *grads = pl.pallas_call(
        functools.partial(feed_body, block=count // 3, direct=direct),
        grid=(4,),
        in_specs=[whole, whole, *specs],
        out_specs=[column, column] + [anywhere] * len(goals),
        out_shape=[jax.ShapeDtypeStruct((count, hidden), BF)] * 2 + goals,
        scratch_shapes=[pltpu.VMEM((width, count), BF)]
        + [pltpu.VMEM((2, *shape), BF) for shape in made]
        + [pltpu.SemaphoreType.DMA((2, 2))],
        compiler_params=pltpu.CompilerParams(
            dimension_semantics=("arbitrary",), vmem_limit_bytes=VMEM_BYTES
        ),
        cost_estimate=pl.CostEstimate(
            flops=8 * count * width * hidden,
            transcendentals=2 * count * hidden,
            bytes_accessed=4 * (count + 2 * width) * (hidden + width),
        ),
    )(h, dy, *weights)
    if direct:
        return f, da, grads[0]
    down, up = grads
    up = up.reshape(owners, part, 4, width).transpose(0, 2, 1, 3)
    packed = jnp.concatenate(
        [down.reshape(owners, 4 * part, width), up.reshape(owners, 4 * part, width)], 1
    )
    return f, da, packed


def turn(x, tables, sign=1.0):
    cosine, ahead, behind = tables
    half = ROT // 2
    return (
        x * cosine
        + pltpu.roll(x, 2 * HD - half, 1) * (sign * ahead)
        + pltpu.roll(x, half, 1) * (sign * behind)
    )


def key_only(tables):
    cosine, ahead, behind = tables
    first = lax.broadcasted_iota(jnp.int32, cosine.shape, 1) < HD
    return jnp.where(first, cosine, 1.0), jnp.where(first, ahead, 0.0), jnp.where(first, behind, 0.0)


def turn_tables(first, count):
    cosine, sine = angles(first, count)
    half = ROT // 2
    rest = jnp.zeros((count, HD - ROT), F32)
    none = jnp.zeros((count, half), F32)
    cosine = jnp.concatenate([cosine, rest + 1.0], 1)
    ahead = jnp.concatenate([-sine[:, :half], none, rest], 1)
    behind = jnp.concatenate([none, sine[:, half:], rest], 1)
    return [jnp.concatenate([t, t], 1) for t in (cosine, ahead, behind)]


def normed_rows(x):
    mean = jnp.mean(x, -1, keepdims=True)
    centered = x - mean
    scale = lax.rsqrt(jnp.mean(centered * centered, -1, keepdims=True) + EPS_NORM)
    return centered * scale, scale


def norm_rows_of(small_ref):
    return small_ref[:, pl.ds(2 * HD, 2 * HD)].astype(F32).T


def entry_body(x_ref, small_ref, cos_ref, ahead_ref, behind_ref, h1_ref, h2_ref, kv_ref, *, block):
    params = norm_rows_of(small_ref)
    weight = small_ref[:, pl.ds(0, 2 * HD)]
    for r in range(0, x_ref.shape[1], block):
        rows = pl.ds(r, block)
        normed, _ = normed_rows(x_ref[0, rows, :].astype(F32))
        first = (normed * params[0:1] + params[1:2]).astype(BF)
        h1_ref[0, rows, :] = first
        h2_ref[0, rows, :] = (normed * params[2:3] + params[3:4]).astype(BF)
        pair = jnp.dot(first, weight, preferred_element_type=F32)
        tables = key_only([t[rows, :] for t in (cos_ref, ahead_ref, behind_ref)])
        kv_ref[0, rows, :] = turn(pair, tables).astype(BF)


def entry(x, small, tables):
    batch, local, width = x.shape
    rows = pl.BlockSpec((1, local, width), lambda b: (b, 0, 0))
    table = pl.BlockSpec((local, 2 * HD), lambda b: (0, 0))
    return pl.pallas_call(
        functools.partial(entry_body, block=local // 3),
        grid=(batch,),
        in_specs=[rows, pl.BlockSpec(small.shape, lambda b: (0, 0)), table, table, table],
        out_specs=[rows, rows, pl.BlockSpec((1, local, 2 * HD), lambda b: (b, 0, 0))],
        out_shape=[jax.ShapeDtypeStruct(x.shape, BF)] * 2
        + [jax.ShapeDtypeStruct((batch, local, 2 * HD), BF)],
        compiler_params=pltpu.CompilerParams(
            dimension_semantics=("arbitrary",), vmem_limit_bytes=VMEM_BYTES
        ),
        cost_estimate=pl.CostEstimate(
            flops=4 * batch * local * width * HD,
            transcendentals=batch * local,
            bytes_accessed=8 * batch * local * width,
        ),
    )(x, small, *tables)


def query_body(h_ref, dy_ref, weight_ref, cos_ref, ahead_ref, behind_ref, q_ref, do_ref):
    mixed = jnp.dot(h_ref[0], weight_ref[:, pl.ds(0, D)], preferred_element_type=F32)
    tables = cos_ref[...], ahead_ref[...], behind_ref[...]
    for c in range(0, D, 2 * HD):
        q = turn(mixed[:, c : c + 2 * HD], tables).astype(BF)
        q_ref[0, :, pl.ds(c, 2 * HD)] = q * BF(HD ** (-0.5))
    do_ref[0] = lax.dot_general(
        dy_ref[0], weight_ref[:, pl.ds(D, D)], COLS_LAST, preferred_element_type=F32
    ).astype(BF)


def queries(h, dy, middle, tables):
    batch, local, width = h.shape
    rows = pl.BlockSpec((1, local, width), lambda b: (b, 0, 0))
    table = pl.BlockSpec((local, 2 * HD), lambda b: (0, 0))
    return pl.pallas_call(
        query_body,
        grid=(batch,),
        in_specs=[rows, rows, pl.BlockSpec(middle.shape, lambda b: (0, 0)), table, table, table],
        out_specs=[rows, rows],
        out_shape=[jax.ShapeDtypeStruct(h.shape, BF)] * 2,
        compiler_params=pltpu.CompilerParams(
            dimension_semantics=("arbitrary",), vmem_limit_bytes=VMEM_BYTES
        ),
        cost_estimate=pl.CostEstimate(
            flops=4 * batch * local * width * width,
            transcendentals=0,
            bytes_accessed=8 * batch * local * width,
        ),
    )(h, dy, middle, *tables)


def back_body(
    core_of, weight_of, x_ref, cot_ref, h_ref, o_ref, dq_ref, dh2_ref, middle_ref, small_ref,
    cos_ref, ahead_ref, behind_ref, *refs, devices,
):
    pair_refs, refs = refs[: devices * weight_of.shape[0]], refs[devices * weight_of.shape[0] :]
    dx_ref, *grad_refs, acc, norm_acc, pair_acc = refs
    b, last = pl.program_id(0), pl.num_programs(0) - 1
    tables = cos_ref[...], ahead_ref[...], behind_ref[...]
    params = norm_rows_of(small_ref)
    dy = cot_ref[0].astype(F32) * weight_of[b]
    dy_low = dy.astype(BF)
    for at in range(weight_of.shape[0]):

        @pl.when(b == at)
        def _(parts=pair_refs[devices * at : devices * (at + 1)]):
            total = parts[0][...].astype(F32)
            for part in parts[1:]:
                total = total + part[...].astype(F32)
            pair_acc[...] = total.astype(BF).astype(F32)

    pair = turn(pair_acc[...], key_only(tables), -1.0).astype(BF)
    turned = [
        turn(dq_ref[0, :, pl.ds(c, 2 * HD)].astype(F32), tables, -1.0).astype(BF)
        for c in range(0, D, 2 * HD)
    ]
    dz = jnp.concatenate(turned + [pair], 1)
    wide = dz.shape[1]
    made = lax.dot_general(h_ref[0], dz, ROWS_FIRST, preferred_element_type=F32)
    made_out = lax.dot_general(o_ref[0], dy_low, ROWS_FIRST, preferred_element_type=F32)

    @pl.when(b == 0)
    def _():
        acc[:, pl.ds(0, wide)] = made
        acc[:, pl.ds(wide, D)] = made_out
        norm_acc[...] = jnp.zeros_like(norm_acc)

    @pl.when(b > 0)
    def _():
        acc[:, pl.ds(0, wide)] += made
        acc[:, pl.ds(wide, D)] += made_out

    weights = jnp.concatenate([middle_ref[:, pl.ds(0, D)], small_ref[:, pl.ds(0, 2 * HD)]], 1)
    dh1 = lax.dot_general(dz, weights, COLS_LAST, preferred_element_type=F32)
    dh2 = dh2_ref[0]
    normed, scale = normed_rows(x_ref[0].astype(F32))
    norm_acc[0:1] += jnp.sum(dh1 * normed, 0, keepdims=True)
    norm_acc[1:2] += jnp.sum(dh1, 0, keepdims=True)
    norm_acc[2:3] += jnp.sum(dh2 * normed, 0, keepdims=True)
    norm_acc[3:4] += jnp.sum(dh2, 0, keepdims=True)
    inner = dh1 * params[0:1] + dh2 * params[2:3]
    inner = inner - jnp.mean(inner, -1, keepdims=True) - normed * jnp.mean(
        inner * normed, -1, keepdims=True
    )
    dx_ref[0] = (dy + scale * inner).astype(BF)

    @pl.when(b == last)
    def _():
        acc[:, pl.ds(wide + D, 2 * HD)] = norm_acc[...].T
        if len(grad_refs) == 1:
            grad_refs[0][...] = acc[...].astype(BF)
            return
        send_ref, keep_ref = grad_refs
        pairs, part, _ = send_ref.shape
        for p in range(pairs):
            for ref, core in ((send_ref, 1 - core_of[0]), (keep_ref, core_of[0])):
                rows = pl.ds(pl.multiple_of((2 * p + core) * part, part), part)
                ref[p] = acc[rows, :].astype(ref.dtype)


def back(core, row_weight, owners, x, cot, h, o, dq, pairs, dh2, middle, small, tables):
    batch, local, width = x.shape
    rows = pl.BlockSpec((1, local, width), lambda b, *s: (b, 0, 0))
    table = pl.BlockSpec((local, 2 * HD), lambda b, *s: (0, 0))
    columns = 2 * width + 4 * HD
    part = width // owners
    if part % 16 == 0:
        half = (owners // 2, part, columns)
        made = [jax.ShapeDtypeStruct(half, BF), jax.ShapeDtypeStruct(half, F32)]
    else:
        made = [jax.ShapeDtypeStruct((width, columns), BF)]
    return pl.pallas_call(
        functools.partial(back_body, devices=len(pairs[0])),
        grid_spec=pltpu.PrefetchScalarGridSpec(
            num_scalar_prefetch=2,
            grid=(batch,),
            in_specs=[rows] * 6
            + [pl.BlockSpec(w.shape, lambda b, *s: (0, 0)) for w in (middle, small)]
            + [table] * (3 + sum(len(parts) for parts in pairs)),
            out_specs=[rows]
            + [pl.BlockSpec(m.shape, lambda b, *s, n=len(m.shape): (0,) * n) for m in made],
            scratch_shapes=[
                pltpu.VMEM((width, columns), F32),
                pltpu.VMEM((2 * HD, width), F32),
                pltpu.VMEM((local, 2 * HD), F32),
            ],
        ),
        out_shape=[jax.ShapeDtypeStruct(x.shape, BF), *made],
        compiler_params=pltpu.CompilerParams(
            dimension_semantics=("arbitrary",), vmem_limit_bytes=VMEM_BYTES
        ),
        cost_estimate=pl.CostEstimate(
            flops=6 * batch * local * width * width,
            transcendentals=batch * local,
            bytes_accessed=16 * batch * local * width,
        ),
    )(
        core, row_weight, x, cot, h, o, dq, dh2, middle, small, *tables,
        *[part for parts in pairs for part in parts],
    )


def sum_body(a_ref, w_ref, out_ref):
    width = out_ref.shape[1]
    part = lax.dot_general(
        a_ref[...], w_ref[...].reshape(width, width), COLS_LAST, preferred_element_type=F32
    )

    @pl.when(pl.program_id(0) == 0)
    def _():
        out_ref[...] = part

    @pl.when(pl.program_id(0) > 0)
    def _():
        out_ref[...] += part


def up_back(da, weights, specs):
    count, hidden = da.shape
    width = hidden // 4
    return pl.pallas_call(
        sum_body,
        grid=(4,),
        in_specs=[pl.BlockSpec((count, width), lambda c: (0, c)), specs[0]],
        out_specs=pl.BlockSpec((count, width), lambda c: (0, 0)),
        out_shape=jax.ShapeDtypeStruct((count, width), F32),
        compiler_params=pltpu.CompilerParams(
            dimension_semantics=("arbitrary",), vmem_limit_bytes=VMEM_BYTES
        ),
        cost_estimate=pl.CostEstimate(
            flops=2 * count * width * hidden,
            transcendentals=0,
            bytes_accessed=2 * count * hidden + 4 * count * width + 2 * width * hidden,
        ),
    )(da, weights[0])


def output_body(x_ref, o_ref, out_w_ref, f_ref, w_ref, y_ref, acc):
    step, last = pl.program_id(0), pl.num_programs(0) - 1
    width = acc.shape[1]
    part = jnp.dot(f_ref[...], w_ref[...].reshape(width, width), preferred_element_type=F32)

    @pl.when(step == 0)
    def _():
        heads = jnp.dot(o_ref[...], out_w_ref[...], preferred_element_type=F32)
        acc[...] = x_ref[...].astype(F32) + heads + part

    @pl.when(step > 0)
    def _():
        acc[...] += part

    @pl.when(step == last)
    def _():
        y_ref[...] = acc[...].astype(BF)


def output(x, o, middle, f, weights, specs):
    count, hidden = f.shape
    width = hidden // 4
    whole = pl.BlockSpec((count, width), lambda c: (0, 0))
    return pl.pallas_call(
        output_body,
        grid=(4,),
        in_specs=[
            whole,
            whole,
            pl.BlockSpec((width, width), lambda c: (0, 1)),
            pl.BlockSpec((count, width), lambda c: (0, c)),
            specs[1],
        ],
        out_specs=whole,
        out_shape=jax.ShapeDtypeStruct((count, width), BF),
        scratch_shapes=[pltpu.VMEM((count, width), F32)],
        compiler_params=pltpu.CompilerParams(
            dimension_semantics=("arbitrary",), vmem_limit_bytes=VMEM_BYTES
        ),
        cost_estimate=pl.CostEstimate(
            flops=2 * count * width * (hidden + width),
            transcendentals=0,
            bytes_accessed=2 * (count + width) * hidden + 6 * count * width,
        ),
    )(x, o, middle, f, weights[1])


def adam_store(weight_ref, first_ref, second_ref, grad, outs, rate, decay):
    results = adam_update(weight_ref[...], first_ref[...], second_ref[...], grad, rate, decay)
    for out_ref, result in zip(outs, results):
        out_ref[...] = result


def adam_body(seq_at, factor_ref, up_grad_ref, down_grad_ref, *refs):
    parts, refs, joined = refs[:4], refs[4:-1], refs[-1]
    factor = factor_ref[0, 0]
    qkv, out, up, down, norm = [refs[3 * i : 3 * i + 3] for i in range(5)]
    outs = refs[15:]
    qkv_out, out_out, up_out, down_out, norm_out = [outs[3 * i : 3 * i + 3] for i in range(5)]
    adam_store(*up, up_grad_ref[...].astype(F32) * factor, up_out, RATE_SMALL, DECAY)
    adam_store(*down, down_grad_ref[...].astype(F32) * factor, down_out, RATE_SMALL, DECAY)

    step = pl.program_id(0)

    @pl.when(step == 0)
    def _():
        for mask, ref in enumerate(parts):
            joined[seq_at[0] ^ mask] = unpack_quarter(ref)

    rest = joined[step]
    wide = qkv[0].shape[1]
    adam_store(*qkv, rest[:, :wide] * factor, qkv_out, RATE_SMALL, DECAY)
    adam_store(*out, rest[:, wide : wide + D] * factor, out_out, RATE_LARGE, DECAY)

    @pl.when(step == pl.num_programs(0) - 1)
    def _():
        norms = joined[:, :, pl.ds(wide + D, 2 * HD)].reshape(-1, 2 * HD)
        adam_store(*norm, norms.T[:4] * factor, norm_out, RATE_NORM, 0.0)


def adam_all(seq_at, factor, feed, rest, qkv, out, up, down, norm):
    part, hidden = up[0].shape
    width = hidden // 4
    column = pl.BlockSpec((part, width), lambda c, p: (0, c))
    row = pl.BlockSpec((part, width), lambda c, p: (c, 0))

    def quarter(x):
        return pl.BlockSpec((part // 4, x.shape[1]), lambda c, p: (c, 0))

    def whole(x):
        return pl.BlockSpec(x.shape, lambda c, p: (0, 0))

    states = [*qkv, *out, *up, *down, *norm]
    specs = (
        [quarter(x) for x in qkv + out] + [column] * 3 + [row] * 3 + [whole(x) for x in norm]
    )
    return pl.pallas_call(
        adam_body,
        grid_spec=pltpu.PrefetchScalarGridSpec(
            num_scalar_prefetch=1,
            grid=(4,),
            in_specs=[
                pl.BlockSpec(memory_space=pltpu.SMEM),
                pl.BlockSpec((part, width), lambda c, p: (4 + c, 0)),
                row,
                *[whole(x) for x in rest],
                *specs,
            ],
            out_specs=specs,
            scratch_shapes=[pltpu.VMEM((4, rest[0].shape[0], rest[0].shape[1] - 2 * HD), F32)],
        ),
        out_shape=[jax.ShapeDtypeStruct(x.shape, F32) for x in states],
        compiler_params=pltpu.CompilerParams(
            dimension_semantics=("arbitrary",), vmem_limit_bytes=VMEM_BYTES
        ),
    )(seq_at, factor, feed, feed, *rest, *states)


def swap(x, axis, mask):
    return lax.ppermute(x, axis, [(i, i ^ mask) for i in range(lax.axis_size(axis))])


def local_call(body, at, inputs, shapes, scratch=(), room=VMEM_BYTES // 3):
    return pl.pallas_call(
        body,
        grid_spec=pltpu.PrefetchScalarGridSpec(
            num_scalar_prefetch=1,
            grid=(1,),
            in_specs=[pl.BlockSpec(a.shape, lambda i, p, n=a.ndim: (0,) * n) for a in inputs],
            out_specs=[pl.BlockSpec(s, lambda i, p, n=len(s): (0,) * n) for s, _ in shapes],
            scratch_shapes=list(scratch),
        ),
        out_shape=[jax.ShapeDtypeStruct(s, kind) for s, kind in shapes],
        compiler_params=pltpu.CompilerParams(
            dimension_semantics=("arbitrary",), vmem_limit_bytes=room
        ),
    )(at, *inputs)


def split_chips(at, keep, came, send_left, send_right, keep_left, keep_right):
    x, y = at[0], at[1]
    half = send_left.shape[2]
    left, right = pl.ds(0, half), pl.ds(half, half)
    for i in range(2):
        for ref, block, columns in (
            (send_left, 2 * i + 1 - x, left),
            (keep_left, 2 * i + x, left),
            (send_right, 2 * (1 - y) + i, right),
            (keep_right, 2 * y + i, right),
        ):
            total = keep[block, :, columns] + came[block, :, columns].astype(F32)
            ref[i] = total.astype(ref.dtype)


def split_last(at, left, right, a, b, send_left, send_right, keep_left, keep_right):
    x, y = at[0], at[1]
    for ref, keep, came, block in (
        (send_left, left, a, 1 - y),
        (keep_left, left, a, y),
        (send_right, right, b, 1 - x),
        (keep_right, right, b, x),
    ):
        ref[...] = (keep[block] + came[block].astype(F32)).astype(ref.dtype)


def split_seq(at, left, right, a, b, one, two, three, keep, total):
    half = left.shape[1]
    quarters, rows, _ = total.shape
    total[:, :, pl.ds(0, half)] = (left[...] + a[...].astype(F32)).reshape(quarters, rows, half)
    total[:, :, pl.ds(half, half)] = (right[...] + b[...].astype(F32)).reshape(quarters, rows, half)
    seq = at[2]
    keep[...] = total[seq]
    for mask, ref in ((1, one), (2, two), (3, three)):
        ref[...] = total[seq ^ mask].astype(BF)


def pack_quarter(at, keep, one, two, three, packed):
    total = keep[...]
    for ref in (one, two, three):
        total = total + ref[...].astype(F32)
    wide = total.shape[1]
    packed[:, pl.ds(0, wide)] = total.astype(BF)
    pair = total[:, D : D + 2 * HD]
    packed[:, pl.ds(wide, 2 * HD)] = (pair - pair.astype(BF).astype(F32)).astype(BF)


def unpack_quarter(ref):
    wide = ref.shape[1] - 2 * HD
    pair = pl.ds(D, 2 * HD)
    after = D + 2 * HD
    return jnp.concatenate(
        [
            ref[:, pl.ds(0, D)].astype(F32),
            ref[:, pair].astype(F32) + ref[:, pl.ds(wide, 2 * HD)].astype(F32),
            ref[:, pl.ds(after, wide - after)].astype(F32),
        ],
        1,
    )


def add_squares(at, *refs):
    *quarters, feed, squares = refs
    total = jnp.zeros(squares.shape, F32)
    for grad in [unpack_quarter(ref) for ref in quarters] + [feed[...].astype(F32)]:
        parts = jnp.sum(jnp.square(grad), 0, keepdims=True)
        for c in range(0, grad.shape[1], 2 * HD):
            total = total + parts[:, c : c + 2 * HD]
    squares[...] = total


def beside(sends, work=lambda: (), inputs=()):
    flat, inputs = lax.optimization_barrier(([x for x, _, _ in sends], inputs))
    came = [swap(x, axis, mask) for x, (_, axis, mask) in zip(flat, sends)]
    return lax.optimization_barrier((came, work(*inputs)))


def batch_sum(at, send, keep, work, inputs):
    (came,), _ = beside([(send, "batch", 1)])
    _, r, c = keep.shape
    two, one, quarter = (2, r, c // 2), (r, c // 2), (r // 4, c)
    send_left, send_right, left, right = local_call(
        split_chips, at, [keep, came], [(two, BF), (two, BF), (two, F32), (two, F32)]
    )
    (a, b), _ = beside([(send_left, "batch", 2), (send_right, "batch", 4)])
    send_left, send_right, left, right = local_call(
        split_last, at, [left, right, a, b], [(one, BF), (one, BF), (one, F32), (one, F32)]
    )
    (a, b), _ = beside([(send_left, "batch", 4), (send_right, "batch", 2)])
    *sends, keep = local_call(
        split_seq,
        at,
        [left, right, a, b],
        [(quarter, BF)] * 3 + [(quarter, F32)],
        [pltpu.VMEM((4, *quarter), F32)],
    )
    came, result = beside([(x, "seq", m + 1) for m, x in enumerate(sends)], work, inputs)
    (own,) = local_call(pack_quarter, at, [keep, *came], [((r // 4, c + 2 * HD), BF)])
    came, _ = beside([(own, "seq", mask) for mask in (1, 2, 3)])
    return [own, *came], result


def shift(x, by):
    count = lax.axis_size("seq")
    return lax.ppermute(x, "seq", [(s, s + by) for s in range(count) if 0 <= s + by < count])


def shards(
    tokens,
    cotangent,
    tags,
    loss_weights,
    w_qkv,
    m_qkv,
    v_qkv,
    w_out,
    m_out,
    v_out,
    w_up,
    m_up,
    v_up,
    w_down,
    m_down,
    v_down,
    norm_params,
    m_norm,
    v_norm,
):
    owners = lax.axis_size("batch")
    seq_count = lax.axis_size("seq")
    seq_at = lax.axis_index("seq")
    seq_rows, local, width = tokens.shape
    count = seq_rows * local
    part = w_qkv.shape[0]
    fence = lax.optimization_barrier

    small = jnp.concatenate(
        [w_qkv[:, D:], norm_params.T, jnp.zeros((part, 2 * HD - 4), F32)], 1
    ).astype(BF)
    middle = jnp.concatenate([w_qkv[:, :D], w_out], 1).astype(BF)
    middle, small = fence((middle, small))
    small = lax.all_gather(small, "batch", axis=0, tiled=True)
    middle = lax.all_gather(middle, "batch", axis=0, tiled=True)
    packed = jnp.concatenate([w_down] + [w_up[:, D * i : D * (i + 1)] for i in range(4)], 0)
    packed, small = fence((packed.astype(BF), small))
    packed = lax.all_gather(packed, "batch", axis=0, tiled=True).reshape(owners, 8 * part, D)
    weights, specs = feed_weights(packed)

    tables = turn_tables(seq_at * local, local)
    subsets = jnp.arange(loss_weights.shape[0])
    row_weight = jnp.sum(
        jnp.where(tags[:, None] == subsets[None, :], loss_weights[None, :], 0.0), -1
    )
    grad_low = (cotangent.astype(F32) * row_weight[:, None, None]).astype(BF)

    first_low, second_low, pair = entry(tokens, small, tables)
    query, grad_heads = queries(first_low, grad_low, middle, tables)

    def gather_pair(own):
        return [own] + [shift(own, by) for by in range(1, seq_count)]

    arrived, query = fence((gather_pair(pair[0]), query))
    place = jnp.reshape(seq_at, (1,)).astype(jnp.int32)

    state, came = (), []
    for at in range(seq_rows):
        if at == seq_rows // 2:
            second_low, state = fence((second_low, state))
            active_low, grad_up_pre, grad_feed = feed_forward(
                second_low.reshape(count, D), grad_low.reshape(count, D), weights, specs, owners
            )
            feed_sum = lax.psum_scatter(
                grad_feed.reshape(owners * 8 * part, D), "batch", scatter_dimension=0, tiled=True
            )
            state, grad_up_pre = fence((state, grad_up_pre))
        keys = arrived
        if at + 1 < seq_rows:
            own, keys = fence((pair[at + 1], keys))
            arrived = gather_pair(own)
        heads, grad_query, *grad_pair = attention(place, query, grad_heads, keys, at, state)
        state = heads, grad_query
        came.append([shift(g, -by) if by else g for by, g in enumerate(grad_pair)])
        if at + 1 < seq_rows:
            arrived, state = fence((arrived, state))
    heads, grad_query = state

    grad_up_pre, heads = fence((grad_up_pre, heads))
    grad_second = up_back(grad_up_pre, weights, specs)
    quarter = (-(-part // 4), w_qkv.shape[1] + D + 4 * HD)
    blanks = [jnp.zeros(quarter, BF)] * 4
    came, grad_second, feed_sum, blanks = fence((came, grad_second, feed_sum, blanks))
    feed_sum = lax.psum(feed_sum, "seq")

    def input_side():
        return back(
            jnp.reshape(lax.axis_index("batch") % 2, (1,)),
            row_weight,
            owners,
            tokens,
            cotangent,
            first_low,
            heads,
            grad_query,
            came,
            grad_second.reshape(seq_rows, local, D),
            middle,
            small,
            tables,
        )

    def output_side(x, o, w, f):
        return output(x, o, w, f, weights, specs)

    output_inputs = tokens.reshape(count, D), heads.reshape(count, D), middle, active_low

    if owners == 8 and seq_count == 4:
        batch_at = lax.axis_index("batch")
        at = jnp.stack([(batch_at // 2) % 2, batch_at // 4, seq_at])

        def rest_of_layer(_, carry):
            input_grad, send, keep = input_side()
            parts, layer_out = batch_sum(at, send, keep, output_side, output_inputs)
            return input_grad, layer_out, parts

        unused = (
            second_low,
            query.reshape(count, D),
            blanks,
        )
        once = 1 + jnp.minimum(tags[0], 0)
        input_grad, layer_out, rest = lax.fori_loop(0, once, rest_of_layer, unused)
        feed_sum, rest = fence((feed_sum, rest))
        (squares,) = local_call(
            add_squares, at, [*rest, feed_sum], [((1, 2 * HD), F32)], room=VMEM_BYTES
        )
        total_squares = jnp.sum(lax.all_gather(squares, "batch"))
    else:
        input_grad, rest = input_side()
        layer_out = output_side(*output_inputs)
        rest = lax.psum_scatter(rest.astype(F32), "batch", scatter_dimension=0, tiled=True)
        rest = lax.psum(rest, "seq")
        squares = [jnp.sum(jnp.square(x.astype(F32))) for x in (rest, feed_sum)]
        total_squares = lax.psum(sum(squares), "batch")
    layer_out = layer_out.reshape(seq_rows, local, D)
    grad_norm = jnp.sqrt(total_squares)
    factor = CLIP_NORM / jnp.maximum(grad_norm, CLIP_NORM)
    states = (
        (w_qkv, m_qkv, v_qkv),
        (w_out, m_out, v_out),
        (w_up, m_up, v_up),
        (w_down, m_down, v_down),
        (norm_params, m_norm, v_norm),
    )
    if isinstance(rest, list):
        results = adam_all(at[2:], factor.reshape(1, 1), feed_sum, rest, *states)
    else:
        qkv_width = w_qkv.shape[1]
        down_sum, up_sum = feed_sum[: 4 * part], feed_sum[4 * part :]
        up_sum = up_sum.astype(F32).reshape(4, part, D).transpose(1, 0, 2)
        grads = (
            rest[:, :qkv_width],
            rest[:, qkv_width : qkv_width + D],
            up_sum.reshape(part, 4 * D),
            down_sum.astype(F32),
            rest[:, qkv_width + D : qkv_width + D + 4].T,
        )
        rates = (RATE_SMALL, RATE_LARGE, RATE_SMALL, RATE_SMALL, RATE_NORM)
        decays = (DECAY, DECAY, DECAY, DECAY, 0.0)
        results = []
        for three, grad, rate, decay in zip(states, grads, rates, decays):
            results.extend(adam_update(*three, grad * factor, rate, decay))
    return (layer_out, input_grad, grad_norm, *results)


def solution(mesh):
    in_specs = (
        P("batch", "seq", None),
        P("batch", "seq", None),
        P("batch"),
        P(),
        P("batch", None),
        P("batch", None),
        P("batch", None),
        P("batch", None),
        P("batch", None),
        P("batch", None),
        P("batch", None),
        P("batch", None),
        P("batch", None),
        P("batch", None),
        P("batch", None),
        P("batch", None),
        P(None, "batch"),
        P(None, "batch"),
        P(None, "batch"),
    )
    out_specs = (
        P("batch", "seq", None),
        P("batch", "seq", None),
        P(),
        P("batch", None),
        P("batch", None),
        P("batch", None),
        P("batch", None),
        P("batch", None),
        P("batch", None),
        P("batch", None),
        P("batch", None),
        P("batch", None),
        P("batch", None),
        P("batch", None),
        P("batch", None),
        P(None, "batch"),
        P(None, "batch"),
        P(None, "batch"),
    )
    return jax.shard_map(shards, mesh=mesh, in_specs=in_specs, out_specs=out_specs, check_vma=False)
```
